32 devices in a mesh: ctx: 8 (over z, x), head: 4 (over y, core).
Axes of the slice: x: 2, y: 2, z: 4, core: 2. Of those that a mesh axis runs over, the one named last changes fastest.
Arguments:
- query_rows: bfloat16 [2048, 8192], P('ctx', 'head'), may hold values from -2.5 to 2.5
- key_rows: bfloat16 [2048, 8192], P('ctx', 'head'), may hold values from -2.5 to 2.5
- value_rows: bfloat16 [2048, 8192], P('ctx', 'head'), may hold values from -8 to 8
- frequencies: float32 [64, 256, 128], P('head'), may hold values from -4 to 4
- norm_gain: float32 [8192], P('head'), may hold values from 0.5 to 1.5
- out_grad: bfloat16 [2048, 8192], P('ctx', 'head'), may hold values from -6 to 6
- global_ids: int32 [2], replicated, may hold values from 0 to 31, as said below
Outputs:
- query_grad: bfloat16 [2048, 8192], P('ctx', 'head')
- key_grad: bfloat16 [2048, 8192], P('ctx', 'head')
- value_grad: bfloat16 [2048, 8192], P('ctx', 'head')
- freq_grad: float32 [64, 256, 128], P('head')
- gain_grad: float32 [8192], P('head')
The draws below stay inside these ranges and needn't reach their ends.
Inputs may be any that keep to these rules, and one draw needn't show every extreme that they name: `global_ids`: 2 different block numbers.
All inputs are finite; a program needn't handle non-finite values.
Results may differ from the reference program's by a relative error of at most 0.029.
Values may be sent and summed in bfloat16 or wider, within the bound.
No kernel may reach another device: no remote copies, remote signals or barrier semaphores. Data moves between devices by JAX's collectives and lax.ppermute only.
A program may use at most 192 MiB of HBM per device.

```python
import jax
import jax.numpy as jnp
from jax import lax

HEADS = 64
DH = 128
D = 8192
M = 256
WIN = 4
G = 2
BLK = 64
NB = 32
TOKENS = 2048


def draw_value_rows(key, part):
    column = jnp.arange(D) // DH
    rising = 0.5 * jnp.power(3.0, column.astype(jnp.float32) / (HEADS - 1))
    base = jax.random.truncated_normal(key, -4.0, 4.0, (TOKENS, D), jnp.float32)
    return (base * rising).astype(jnp.bfloat16)


def draw_global_ids(key, part):
    order = jax.random.permutation(key, NB)
    return order[:G].astype(jnp.int32)


def shard_levels(rng, extent, split, low, top_value):
    gain, own = 1.0, jax.random.fold_in(rng, 6)
    for position, blocks in split:
        steps = jnp.exp(jax.random.uniform(jax.random.fold_in(own, position), (blocks,), jnp.float32, low / len(split), top_value / len(split)))
        gain = gain * jnp.repeat(steps, extent[position] // blocks).reshape([-1 if axis == position else 1 for axis in range(len(extent))])
    return gain


def centred(own_key, shape, scale, most, pieces=(), held_as=jnp.bfloat16):
    loudness = shard_levels(own_key, shape, pieces, -0.22, 0.18) if pieces else 1.0
    array = jax.random.normal(own_key, shape, jnp.float32) * scale * loudness
    return jnp.minimum(jnp.maximum(array, -most), most).astype(held_as)


def setup_inputs(seed: int = 0) -> dict:
    streams_of = jax.random.split(jax.random.key(seed), 8)
    return {
        "query_rows": centred(streams_of[0], (TOKENS, D), 0.5, 2.5, ((0, 8), (1, 4))),
        "key_rows": centred(streams_of[1], (TOKENS, D), 0.5, 2.5, ((0, 8), (1, 4))),
        "value_rows": draw_value_rows(jax.random.fold_in(streams_of[7], 71), 0),
        "frequencies": centred(streams_of[3], (HEADS, M, DH), 1.0, 4.0, ((0, 4),), jnp.float32),
        "norm_gain": jnp.clip(1.0 + 0.1 * jax.random.normal(streams_of[4], (D,), jnp.float32), 0.5, 1.5),
        "out_grad": centred(streams_of[5], (TOKENS, D), 1.0, 6.0, ((0, 8), (1, 4))),
        "global_ids": draw_global_ids(jax.random.fold_in(streams_of[7], 71), 0),
    }


EPS = 1e-05
HIGH = lax.Precision.HIGHEST

def rounded(values):
    return lax.optimization_barrier(values.astype(jnp.bfloat16))

def feature_map(row_entries, frequency_lowprec, feat_scale):
    score_matrix = jnp.dot(row_entries, frequency_lowprec.T, preferred_element_type=jnp.float32)
    square = lax.optimization_barrier(jnp.sum(jnp.square(row_entries.astype(jnp.float32)), axis=-1, keepdims=True))
    return jnp.exp(feat_scale * score_matrix - 0.5 * feat_scale * feat_scale * square) * M ** (-0.5)

def attend_pattern(global_ids):
    query_block = jnp.arange(NB, dtype=jnp.int32)[:, None]
    key_block = jnp.arange(NB, dtype=jnp.int32)[None, :]
    nearby = (key_block > query_block - WIN) & (key_block <= query_block)
    chosen = jnp.any(jnp.arange(NB, dtype=jnp.int32)[:, None] == global_ids[None, :].astype(jnp.int32), axis=1)
    return (nearby | chosen[None, :]).astype(jnp.float32)

def head_forward(query_head, key_head, value_head, frequency_lowprec, allowed):
    feat_scale = DH ** (-0.25)
    query_feat = feature_map(query_head, frequency_lowprec, feat_scale)
    key_feat = feature_map(key_head, frequency_lowprec, feat_scale)
    query_low = rounded(query_feat)
    key_low = rounded(key_feat)
    key_blocks = key_low.reshape(NB, BLK, M).astype(jnp.float32)
    value_blocks = value_head.reshape(NB, BLK, DH).astype(jnp.float32)
    summary = jnp.einsum('ntm,ntd->nmd', key_blocks, value_blocks)
    key_sum = lax.optimization_barrier(jnp.sum(key_feat.reshape(NB, BLK, M), axis=1))
    total = jnp.einsum('bc,cmd->bmd', allowed, summary, precision=HIGH)
    total_sum = jnp.dot(allowed, key_sum, precision=HIGH)
    total_low = rounded(total).astype(jnp.float32)
    query_blocks = query_low.reshape(NB, BLK, M).astype(jnp.float32)
    numerator = jnp.einsum('btm,bmd->btd', query_blocks, total_low)
    denominator = jnp.einsum('btm,bm->bt', query_feat.reshape(NB, BLK, M), total_sum, precision=HIGH)
    attended = (numerator / denominator[..., None]).reshape(TOKENS, DH)
    return (attended, denominator.reshape(TOKENS), query_feat, key_feat, query_blocks, key_blocks, value_blocks, total_low, total_sum)

def reference(query_rows, key_rows, value_rows, frequencies, norm_gain, out_grad, global_ids):
    allowed = attend_pattern(global_ids)
    feat_scale = DH ** (-0.25)

    def split_heads(row_entries):
        return row_entries.reshape(TOKENS, HEADS, DH).transpose(1, 0, 2)
    query_head_stack = split_heads(query_rows)
    key_head_stack = split_heads(key_rows)
    value_heads = split_heads(value_rows)
    grad_heads = split_heads(out_grad)
    freq_lows = frequencies.astype(jnp.bfloat16)
    gain_heads = norm_gain.reshape(HEADS, DH)

    def first_pass(inputs):
        query_head, key_head, value_head, grad_head, frequency_lowprec, gain_head = inputs
        attended = head_forward(query_head, key_head, value_head, frequency_lowprec, allowed)[0]
        squares = lax.optimization_barrier(jnp.sum(jnp.square(attended), axis=1))
        product = lax.optimization_barrier(jnp.sum(gain_head[None, :] * grad_head.astype(jnp.float32) * attended, axis=1))
        return (squares, product)
    stacked = (query_head_stack, key_head_stack, value_heads, grad_heads, freq_lows, gain_heads)
    squares_all, product_all = lax.map(first_pass, stacked)
    norm_inv = lax.rsqrt(lax.optimization_barrier(jnp.sum(squares_all, axis=0)) / D + EPS)
    product = lax.optimization_barrier(jnp.sum(product_all, axis=0))

    def second_pass(inputs):
        query_head, key_head, value_head, grad_head, frequency_lowprec, gain_head = inputs
        attended, denominator, query_feat, key_feat, query_blocks, key_blocks, value_blocks, total_low, total_sum = head_forward(query_head, key_head, value_head, frequency_lowprec, allowed)
        grad_float = grad_head.astype(jnp.float32)
        attended_grad = norm_inv[:, None] * gain_head[None, :] * grad_float - attended * (norm_inv ** 3 * product / D)[:, None]
        gain_part = lax.optimization_barrier(jnp.sum(grad_float * attended * norm_inv[:, None], axis=0))
        numerator_grad = rounded(attended_grad / denominator[:, None]).astype(jnp.float32)
        denominator_grad = -lax.optimization_barrier(jnp.sum(attended_grad * attended, axis=1)) / denominator
        numer_blocks = numerator_grad.reshape(NB, BLK, DH)
        denom_blocks = denominator_grad.reshape(NB, BLK)
        query_feat_grad = jnp.einsum('btd,bmd->btm', numer_blocks, total_low) + denom_blocks[..., None] * total_sum[:, None, :]
        total_grad = jnp.einsum('btm,btd->bmd', query_blocks, numer_blocks)
        total_sum_grad = jnp.einsum('btm,bt->bm', query_feat.reshape(NB, BLK, M), denom_blocks, precision=HIGH)
        summary_grad = jnp.einsum('bc,bmd->cmd', allowed, total_grad, precision=HIGH)
        key_sum_grad = jnp.einsum('bc,bm->cm', allowed, total_sum_grad, precision=HIGH)
        summary_low = rounded(summary_grad).astype(jnp.float32)
        key_feat_grad = (jnp.einsum('ntd,nmd->ntm', value_blocks, summary_low) + key_sum_grad[:, None, :]).reshape(TOKENS, M)
        value_grad = jnp.einsum('ntm,nmd->ntd', key_blocks, summary_low).reshape(TOKENS, DH).astype(jnp.bfloat16)
        query_u = query_feat_grad.reshape(TOKENS, M) * query_feat
        key_u = key_feat_grad * key_feat
        query_projection_lowprec = rounded(query_u)
        key_projection_lowprec = rounded(key_u)
        query_grad = (feat_scale * jnp.dot(query_projection_lowprec, frequency_lowprec, preferred_element_type=jnp.float32) - feat_scale * feat_scale * query_head.astype(jnp.float32) * lax.optimization_barrier(jnp.sum(query_u, axis=1, keepdims=True))).astype(jnp.bfloat16)
        key_grad = (feat_scale * jnp.dot(key_projection_lowprec, frequency_lowprec, preferred_element_type=jnp.float32) - feat_scale * feat_scale * key_head.astype(jnp.float32) * lax.optimization_barrier(jnp.sum(key_u, axis=1, keepdims=True))).astype(jnp.bfloat16)
        freq_part = feat_scale * (jnp.dot(query_projection_lowprec.T, query_head, preferred_element_type=jnp.float32) + jnp.dot(key_projection_lowprec.T, key_head, preferred_element_type=jnp.float32))
        return (query_grad, key_grad, value_grad, freq_part, gain_part)
    query_all, key_all, value_all, freq_grad, gain_all = lax.map(second_pass, stacked)

    def join_heads(row_entries):
        return row_entries.transpose(1, 0, 2).reshape(TOKENS, D)
    return (join_heads(query_all), join_heads(key_all), join_heads(value_all), freq_grad, gain_all.reshape(D))
```

```python
import functools

import jax
import jax.numpy as jnp
from jax import lax
from jax.experimental import pallas as pl
from jax.experimental.pallas import tpu as pltpu
from jax.sharding import PartitionSpec as P

D = 8192
BPD = 4
WIN = 4
EPS = 1e-05
BF = jnp.bfloat16
F32 = jnp.float32


def nt(a, b):
    return lax.dot_general(a, b, (((1,), (1,)), ((), ())), preferred_element_type=F32)


def nn(a, b):
    return lax.dot_general(a, b, (((1,), (0,)), ((), ())), preferred_element_type=F32)


def tn(a, b):
    return lax.dot_general(a, b, (((0,), (0,)), ((), ())), preferred_element_type=F32)


def feats(rows, freq):
    scale = rows.shape[-1] ** (-0.25)
    wide = rows.astype(F32)
    square = jnp.sum(wide * wide, axis=-1, keepdims=True)
    score = nt(rows, freq)
    return (
        jnp.exp(scale * score - (0.5 * scale * scale) * square) * freq.shape[0] ** (-0.5)
    ).astype(BF)


def block_of(shape, axis, length):
    return lax.broadcasted_iota(jnp.int32, shape, axis) // length


def own_mask(n, blk):
    return block_of((n, n), 0, blk) <= block_of((n, n), 1, blk)


def prev_mask(m, n, blk, pos):
    return (block_of((m, n), 0, blk) >= block_of((m, n), 1, blk)) & (pos > 0)


def glob_mask(m, n, blk, pos, ids):
    which = block_of((m, n), 0, blk)
    target = jnp.where(which == 0, ids[0], ids[1])
    query = block_of((m, n), 1, blk) + pos * BPD
    return (target > query) | (target <= query - WIN)


def next_mask(n, m, blk, pos, last):
    return (block_of((n, m), 0, blk) >= block_of((n, m), 1, blk) + 1) & (pos < last)


def feat_kernel(q_ref, k_ref, f_ref, qf_ref, kf_ref):
    freq = f_ref[0].astype(BF)
    qf_ref[0] = feats(q_ref[...], freq)
    kf_ref[0] = feats(k_ref[...], freq)


def masked_scores(kf, kfp, kfg, qf, blk, pos, ids):
    n = qf.shape[0]
    own = jnp.where(own_mask(n, blk), nt(kf, qf), 0.0)
    prev = jnp.where(prev_mask(kfp.shape[0], n, blk, pos), nt(kfp, qf), 0.0)
    glob = jnp.where(glob_mask(kfg.shape[0], n, blk, pos, ids), nt(kfg, qf), 0.0)
    return own, prev, glob


def forward_kernel(
    sc_ref, qf_ref, kf_ref, kp_ref, kg_ref, v_ref, vp_ref, vg_ref, f_ref, g_ref, gain_ref,
    att_ref, kfp_ref, kfg_ref, rows_ref,
):
    freq = f_ref[0].astype(BF)
    kfp = feats(kp_ref[...], freq)
    kfg = feats(kg_ref[...], freq)
    kfp_ref[0] = kfp
    kfg_ref[0] = kfg
    qf = qf_ref[0]
    blk = qf.shape[0] // BPD
    own, prev, glob = masked_scores(
        kf_ref[0], kfp, kfg, qf, blk, sc_ref[0], (sc_ref[1], sc_ref[2])
    )
    den = (
        jnp.sum(own, axis=0, keepdims=True)
        + jnp.sum(prev, axis=0, keepdims=True)
        + jnp.sum(glob, axis=0, keepdims=True)
    )
    num = (
        tn(v_ref[...], own.astype(BF))
        + tn(vp_ref[...], prev.astype(BF))
        + tn(vg_ref[...], glob.astype(BF))
    )
    att = num / den
    gg = (gain_ref[...] * g_ref[...].astype(F32)).T
    att_ref[0] = att
    rows_ref[0, 0:1, :] = den
    rows_ref[0, 1:2, :] = jnp.sum(att * att, axis=0, keepdims=True)
    rows_ref[0, 2:3, :] = jnp.sum(att * gg, axis=0, keepdims=True)
    rows_ref[0, 3:8, :] = jnp.zeros((5, den.shape[1]), F32)


def norm_kernel(ab_ref, rows_ref, att_ref, g_ref, gain_ref, ng_ref, ngs_ref, dg_ref, gp_ref):
    alpha = ab_ref[0:1, :]
    beta = ab_ref[1:2, :]
    den = rows_ref[0, 0:1, :]
    att = att_ref[0]
    wide = g_ref[...].astype(F32)
    gg = (gain_ref[...] * wide).T
    grad = alpha * gg - att * beta
    ng = (grad / den).T.astype(BF)
    ng_ref[...] = ng
    ngs_ref[...] = ng[: ngs_ref.shape[0]]
    dg_ref[0] = -(alpha * rows_ref[0, 2:3, :] - beta * rows_ref[0, 1:2, :]) / den
    normed = (att * alpha).T
    gp_ref[0] = jnp.sum(wide * normed, axis=0, keepdims=True)


def row_grad(u, low, rows, freq, scale):
    return scale * nn(low, freq) - (scale * scale) * rows.astype(F32) * jnp.sum(
        u, axis=-1, keepdims=True
    )


def backward_kernel(
    sc_ref, q_ref, k_ref, kp_ref, kg_ref, v_ref, vp_ref, vg_ref, qf_ref, kf_ref, kfp_ref, kfg_ref,
    ng_ref, dg_ref, gp_ref, f_ref,
    qg_ref, kpart_ref, vpart_ref, z_ref,
):
    freq = f_ref[0].astype(BF)
    scale = freq.shape[1] ** (-0.25)
    qf, kf, kfp, kfg = qf_ref[0], kf_ref[0], kfp_ref[0], kfg_ref[0]
    n = qf.shape[0]
    blk = n // BPD
    pos = sc_ref[0]
    ids = (sc_ref[1], sc_ref[2])
    own, prev, glob = masked_scores(kf, kfp, kfg, qf, blk, pos, ids)
    ng = ng_ref[...]
    dg = dg_ref[0]
    vpart_ref[...] = nn(own.astype(BF), ng)
    vglob = nn(glob.astype(BF), ng)
    d_own = jnp.where(own_mask(n, blk), nt(v_ref[...], ng) + dg, 0.0).astype(BF)
    d_prev = jnp.where(
        prev_mask(kfp.shape[0], n, blk, pos), nt(vp_ref[...], ng) + dg, 0.0
    ).astype(BF)
    d_glob = jnp.where(
        glob_mask(kfg.shape[0], n, blk, pos, ids), nt(vg_ref[...], ng) + dg, 0.0
    ).astype(BF)
    qu = (tn(d_own, kf) + tn(d_prev, kfp) + tn(d_glob, kfg)) * qf.astype(F32)
    ku = nn(d_own, qf) * kf.astype(F32)
    kup = nn(d_prev, qf) * kfp.astype(F32)
    kug = nn(d_glob, qf) * kfg.astype(F32)
    qul, kul, kupl, kugl = qu.astype(BF), ku.astype(BF), kup.astype(BF), kug.astype(BF)
    q, k, kp, kg = q_ref[...], k_ref[...], kp_ref[...], kg_ref[...]
    qg_ref[...] = row_grad(qu, qul, q, freq, scale).astype(BF)
    kpart_ref[...] = row_grad(ku, kul, k, freq, scale)
    m = freq.shape[0]
    ngl = kg.shape[0]
    z_ref[0, 0:m, :] = (scale * (tn(qul, q) + tn(kul, k) + tn(kupl, kp) + tn(kugl, kg))).astype(BF)
    z_ref[0, m : m + ngl, :] = row_grad(kug, kugl, kg, freq, scale).astype(BF)
    z_ref[0, m + ngl : m + 2 * ngl, :] = vglob.astype(BF)
    z_ref[0, m + 2 * ngl :, :] = jnp.broadcast_to(gp_ref[0], (16, freq.shape[1])).astype(BF)


def next_kernel(sc_ref, qn_ref, ngn_ref, dgn_ref, k_ref, v_ref, kf_ref, f_ref, kpart_ref, vpart_ref,
                kg_ref, vg_ref):
    freq = f_ref[0].astype(BF)
    scale = freq.shape[1] ** (-0.25)
    qf = feats(qn_ref[...], freq)
    kf = kf_ref[0]
    n, m = kf.shape[0], qf.shape[0]
    mask = next_mask(n, m, n // BPD, sc_ref[0], sc_ref[3])
    ng = ngn_ref[...]
    pt = jnp.where(mask, nt(kf, qf), 0.0).astype(BF)
    dt = jnp.where(mask, nt(v_ref[...], ng) + dgn_ref[0][:, :m], 0.0).astype(BF)
    vg_ref[...] = vpart_ref[...] + nn(pt, ng)
    ku = nn(dt, qf) * kf.astype(F32)
    kg_ref[...] = kpart_ref[...] + row_grad(ku, ku.astype(BF), k_ref[...], freq, scale)


def add_kernel(sc_ref, kpart_ref, vpart_ref, z_ref, kg_ref, vg_ref, fq_ref, gp_ref):
    m = fq_ref.shape[1]
    n = kpart_ref.shape[0]
    blk = n // BPD
    pos = sc_ref[0]
    fq_ref[0] = z_ref[0, 0:m, :].astype(F32)
    k0 = z_ref[0, m : m + blk, :].astype(F32)
    k1 = z_ref[0, m + blk : m + 2 * blk, :].astype(F32)
    v0 = z_ref[0, m + 2 * blk : m + 3 * blk, :].astype(F32)
    v1 = z_ref[0, m + 3 * blk : m + 4 * blk, :].astype(F32)
    for r in range(BPD):
        here = pos * BPD + r
        w0 = jnp.where(sc_ref[1] == here, 1.0, 0.0).astype(F32)
        w1 = jnp.where(sc_ref[2] == here, 1.0, 0.0).astype(F32)
        rows = slice(r * blk, (r + 1) * blk)
        kg_ref[rows, :] = (kpart_ref[rows, :] + w0 * k0 + w1 * k1).astype(BF)
        vg_ref[rows, :] = (vpart_ref[rows, :] + w0 * v0 + w1 * v1).astype(BF)
    gp_ref[0] = z_ref[0, m + 4 * blk : m + 4 * blk + 1, :].astype(F32)


def head_call(kernel, heads, ins, outs, args, name, flops):
    def spec(kind, array):
        shape = array.shape
        if kind == "s":
            return pl.BlockSpec(memory_space=pltpu.SMEM)
        if kind == "c":
            return pl.BlockSpec((shape[0], shape[1] // heads), lambda h: (0, h))
        if kind == "h":
            return pl.BlockSpec((1,) + shape[1:], lambda h: (h,) + (0,) * (len(shape) - 1))
        return pl.BlockSpec(shape, lambda h: (0,) * len(shape))

    total = sum(a.size * a.dtype.itemsize for a in args) + sum(
        o.size * o.dtype.itemsize for _, o in outs
    )
    return pl.pallas_call(
        kernel,
        grid=(heads,),
        in_specs=[spec(kind, a) for kind, a in zip(ins, args)],
        out_specs=[spec(kind, o) for kind, o in outs],
        out_shape=[o for _, o in outs],
        name=name,
        cost_estimate=pl.CostEstimate(flops=flops, bytes_accessed=total, transcendentals=0),
    )(*args)


def spread(array, count):
    rows = array.shape[0] // count
    parts = lax.all_to_all(array.reshape(count, rows, array.shape[1]), "ctx", 0, 0, tiled=True)
    return jnp.sum(parts.astype(F32), axis=0).astype(array.dtype)


def collect(piece, count):
    parts = jnp.broadcast_to(piece[None], (count,) + piece.shape)
    return lax.all_to_all(parts, "ctx", 0, 0, tiled=True).reshape(-1, piece.shape[1])


def local(query_rows, key_rows, value_rows, frequencies, norm_gain, out_grad, global_ids):
    count = lax.axis_size("ctx")
    pos = lax.axis_index("ctx")
    n, width = query_rows.shape
    heads, m, dh = frequencies.shape
    blk = n // BPD
    reach = (WIN - 1) * blk
    sds = jax.ShapeDtypeStruct
    unit = 2 * heads * n * m * dh
    ids = global_ids.astype(jnp.int32)
    scal = jnp.stack([pos.astype(jnp.int32), ids[0], ids[1], jnp.int32(count - 1)])
    gain = norm_gain.reshape(1, width)
    forth = [(i, i + 1) for i in range(count - 1)]
    back = [(i + 1, i) for i in range(count - 1)]

    kp = lax.ppermute(key_rows[n - reach :], "ctx", forth)
    vp = lax.ppermute(value_rows[n - reach :], "ctx", forth)

    block_ids = pos * BPD + jnp.arange(BPD, dtype=jnp.int32)
    owned = (ids[:, None] == block_ids[None, :]).any(axis=1)
    local_block = jnp.clip(ids - pos * BPD, 0, BPD - 1)

    def pick(rows, g):
        part = lax.dynamic_slice(rows, (local_block[g] * blk, 0), (blk, width))
        return jnp.where(owned[g], part, jnp.zeros_like(part))

    glob = jnp.concatenate(
        [pick(key_rows, 0), pick(key_rows, 1), pick(value_rows, 0), pick(value_rows, 1)], axis=0
    )
    glob = collect(spread(glob, count), count)
    kg, vg = glob[: 2 * blk], glob[2 * blk :]
    qn = lax.ppermute(query_rows[:reach], "ctx", back)

    qf, kf = head_call(
        feat_kernel, heads, "cch",
        [("h", sds((heads, n, m), BF)), ("h", sds((heads, n, m), BF))],
        (query_rows, key_rows, frequencies), "features", 2 * unit,
    )
    att, kfp, kfg, rows = head_call(
        forward_kernel, heads, "shhccccchcc",
        [
            ("h", sds((heads, dh, n), F32)),
            ("h", sds((heads, reach, m), BF)),
            ("h", sds((heads, 2 * blk, m), BF)),
            ("h", sds((heads, 8, n), F32)),
        ],
        (scal, qf, kf, kp, kg, value_rows, vp, vg, frequencies, out_grad, gain),
        "forward", 6 * unit,
    )
    sums = lax.psum(jnp.sum(rows[:, 1:3], axis=0), "head")
    norm_inv = lax.rsqrt(sums[0] / D + EPS)
    beta = norm_inv * norm_inv * norm_inv * sums[1] / D
    ab = jnp.stack([norm_inv, beta])
    ng, ngs, dg, gp = head_call(
        norm_kernel, heads, "ahhcc",
        [
            ("c", sds((n, width), BF)),
            ("c", sds((reach, width), BF)),
            ("h", sds((heads, 1, n), F32)),
            ("h", sds((heads, 1, dh), F32)),
        ],
        (ab, rows, att, out_grad, gain), "norm", unit // 64,
    )
    ngn = lax.ppermute(ngs, "ctx", back)
    dgn = lax.ppermute(dg, "ctx", back)
    qg, kpart, vpart, z = head_call(
        backward_kernel, heads, "s" + "c" * 7 + "hhhhchhh",
        [
            ("c", sds((n, width), BF)),
            ("c", sds((n, width), F32)),
            ("c", sds((n, width), F32)),
            ("h", sds((heads, m + 4 * blk + 16, dh), BF)),
        ],
        (scal, query_rows, key_rows, kp, kg, value_rows, vp, vg, qf, kf, kfp, kfg, ng, dg, gp,
         frequencies),
        "backward", 16 * unit,
    )
    kpart, vpart = head_call(
        next_kernel, heads, "scchcchhcc",
        [("c", sds((n, width), F32)), ("c", sds((n, width), F32))],
        (scal, qn, ngn, dgn, key_rows, value_rows, kf, frequencies, kpart, vpart),
        "following", 5 * unit,
    )
    zrows = m + 4 * blk + 16
    z = collect(spread(z.reshape(heads * zrows, dh), count), count).reshape(heads, zrows, dh)
    kgrad, vgrad, fgrad, gain_grad = head_call(
        add_kernel, heads, "scch",
        [
            ("c", sds((n, width), BF)),
            ("c", sds((n, width), BF)),
            ("h", sds((heads, m, dh), F32)),
            ("h", sds((heads, 1, dh), F32)),
        ],
        (scal, kpart, vpart, z), "finish", unit // 64,
    )
    return (qg, kgrad, vgrad, fgrad, gain_grad.reshape(-1))


def solution(mesh):
    strip = P("ctx", "head")
    return jax.shard_map(
        local,
        mesh=mesh,
        in_specs=(strip, strip, strip, P("head", None, None), P("head"), strip, P()),
        out_specs=(strip, strip, strip, P("head", None, None), P("head")),
        check_vma=False,
    )
```

```python
import jax
import jax.numpy as jnp
from jax import lax
from jax.experimental import pallas as pl
from jax.experimental.pallas import tpu as pltpu
from jax.sharding import PartitionSpec as P

D = 8192
BPD = 4
WIN = 4
EPS = 1e-05
BF = jnp.bfloat16
F32 = jnp.float32
PAD = 16
HB = 2


def nt(a, b):
    return lax.dot_general(a, b, (((1,), (1,)), ((), ())), preferred_element_type=F32)


def nn(a, b):
    return lax.dot_general(a, b, (((1,), (0,)), ((), ())), preferred_element_type=F32)


def tn(a, b):
    return lax.dot_general(a, b, (((0,), (0,)), ((), ())), preferred_element_type=F32)


def feats(rows, freq):
    scale = rows.shape[-1] ** (-0.25)
    wide = rows.astype(F32)
    square = jnp.sum(wide * wide, axis=-1, keepdims=True)
    score = nt(rows, freq)
    return (
        jnp.exp(scale * score - (0.5 * scale * scale) * square) * freq.shape[0] ** (-0.5)
    ).astype(BF)


def block_of(shape, axis, length):
    return lax.broadcasted_iota(jnp.int32, shape, axis) // length


def own_mask(n, blk):
    return block_of((n, n), 0, blk) <= block_of((n, n), 1, blk)


def prev_mask(m, n, blk, pos):
    return (block_of((m, n), 0, blk) >= block_of((m, n), 1, blk)) & (pos > 0)


def glob_mask(m, n, blk, pos, ids):
    which = block_of((m, n), 0, blk)
    target = jnp.where(which == 0, ids[0], ids[1])
    query = block_of((m, n), 1, blk) + pos * BPD
    return (target > query) | (target <= query - WIN)


def next_mask(n, m, blk, pos, last):
    return (block_of((n, m), 0, blk) >= block_of((n, m), 1, blk) + 1) & (pos < last)


def strip(ref, i, dh):
    return ref[:, i * dh : (i + 1) * dh]


def gather_kernel(sc_ref, k_ref, v_ref, kv_ref, glob_ref):
    n = k_ref.shape[0]
    blk = n // BPD
    pos = sc_ref[0]
    reach = n - (BPD - WIN + 1) * blk
    kv_ref[:reach, :] = k_ref[n - reach :, :]
    kv_ref[reach:, :] = v_ref[n - reach :, :]
    for g in range(2):
        at = sc_ref[1 + g] - pos * BPD
        here = (at >= 0) & (at < BPD)
        start = pl.multiple_of(jnp.clip(at, 0, BPD - 1) * blk, blk)
        for i, src in enumerate((k_ref, v_ref)):
            rows = src[pl.ds(start, blk), :]
            first = (2 * i + g) * blk
            glob_ref[0, first : first + blk, :] = jnp.where(here, rows, jnp.zeros_like(rows))


def feat_kernel(sc_ref, q_ref, k_ref, f_ref, qf_ref, kf_ref):
    dh = f_ref.shape[2]
    for i in range(HB):
        freq = f_ref[i].astype(BF)
        qf_ref[i] = feats(strip(q_ref, i, dh), freq)
        kf_ref[i] = feats(strip(k_ref, i, dh), freq)


def masked_scores(kf, kfp, kfg, qf, blk, pos, ids):
    n = qf.shape[0]
    own = jnp.where(own_mask(n, blk), nt(kf, qf), 0.0)
    prev = jnp.where(prev_mask(kfp.shape[0], n, blk, pos), nt(kfp, qf), 0.0)
    glob = jnp.where(glob_mask(kfg.shape[0], n, blk, pos, ids), nt(kfg, qf), 0.0)
    return own, prev, glob


def forward_kernel(
    sc_ref, qf_ref, kf_ref, kv_ref, glob_ref, v_ref, f_ref, g_ref, gain_ref,
    att_ref, kfp_ref, kfg_ref, rows_ref, sums_ref,
):
    dh = f_ref.shape[2]
    n = v_ref.shape[0]
    blk = n // BPD
    reach = kv_ref.shape[0] // 2
    half = glob_ref.shape[2] // 2
    squares = jnp.zeros((1, n), F32)
    products = jnp.zeros((1, n), F32)
    for i in range(HB):
        freq = f_ref[i].astype(BF)
        cols = slice(i * dh, (i + 1) * dh)
        kfp = feats(kv_ref[:reach, cols], freq)
        kfg = feats(glob_ref[0, 0, :half, cols], freq)
        kfp_ref[i] = kfp
        kfg_ref[i] = kfg
        own, prev, glob = masked_scores(
            kf_ref[i], kfp, kfg, qf_ref[i], blk, sc_ref[0], (sc_ref[1], sc_ref[2])
        )
        den = (
            jnp.sum(own, axis=0, keepdims=True)
            + jnp.sum(prev, axis=0, keepdims=True)
            + jnp.sum(glob, axis=0, keepdims=True)
        )
        num = (
            tn(v_ref[:, cols], own.astype(BF))
            + tn(kv_ref[reach:, cols], prev.astype(BF))
            + tn(glob_ref[0, 0, half:, cols], glob.astype(BF))
        )
        att = num / den
        gg = (gain_ref[:, cols] * g_ref[:, cols].astype(F32)).T
        square = jnp.sum(att * att, axis=0, keepdims=True)
        product = jnp.sum(att * gg, axis=0, keepdims=True)
        att_ref[i] = att
        rows_ref[i, 0:1, :] = den
        rows_ref[i, 1:2, :] = square
        rows_ref[i, 2:3, :] = product
        rows_ref[i, 3:8, :] = jnp.zeros((5, n), F32)
        squares += square
        products += product

    @pl.when(pl.program_id(0) == 0)
    def _():
        sums_ref[...] = jnp.zeros_like(sums_ref)

    sums_ref[0:1, :] += squares
    sums_ref[1:2, :] += products


def norm_kernel(
    sc_ref, sums_ref, rows_ref, att_ref, g_ref, gain_ref, ng_ref, ngs_ref, dg_ref, gp_ref
):
    dh = att_ref.shape[1]
    alpha = lax.rsqrt(sums_ref[0:1, :] / D + EPS)
    beta = alpha * alpha * alpha * sums_ref[1:2, :] / D
    reach = ngs_ref.shape[0] - PAD
    for i in range(HB):
        cols = slice(i * dh, (i + 1) * dh)
        den = rows_ref[i, 0:1, :]
        att = att_ref[i]
        wide = g_ref[:, cols].astype(F32)
        gg = (gain_ref[:, cols] * wide).T
        ng = ((alpha * gg - att * beta) / den).T.astype(BF)
        dg = -(alpha * rows_ref[i, 2:3, :] - beta * rows_ref[i, 1:2, :]) / den
        ng_ref[:, cols] = ng
        dg_ref[i] = dg
        ngs_ref[:reach, cols] = ng[:reach]
        pieces = [jnp.broadcast_to(dg[:, j : j + dh], (PAD // 2, dh)) for j in (0, dh)]
        ngs_ref[reach:, cols] = jnp.concatenate(pieces, axis=0).astype(BF)
        gp_ref[i] = jnp.sum(wide * (att * alpha).T, axis=0, keepdims=True)


def row_grad(u, low, rows, freq, scale):
    return scale * nn(low, freq) - (scale * scale) * rows.astype(F32) * jnp.sum(
        u, axis=-1, keepdims=True
    )


def backward_kernel(
    sc_ref, q_ref, k_ref, kv_ref, glob_ref, v_ref, qf_ref, kf_ref, kfp_ref, kfg_ref,
    ng_ref, dg_ref, gp_ref, f_ref,
    qg_ref, kpart_ref, vpart_ref, z_ref,
):
    m, dh = f_ref.shape[1:]
    scale = dh ** (-0.25)
    n = q_ref.shape[0]
    blk = n // BPD
    reach = kv_ref.shape[0] // 2
    ngl = glob_ref.shape[2] // 2
    pos = sc_ref[0]
    ids = (sc_ref[1], sc_ref[2])
    for i in range(HB):
        freq = f_ref[i].astype(BF)
        cols = slice(i * dh, (i + 1) * dh)
        qf, kf, kfp, kfg = qf_ref[i], kf_ref[i], kfp_ref[i], kfg_ref[i]
        own, prev, glob = masked_scores(kf, kfp, kfg, qf, blk, pos, ids)
        ng = ng_ref[:, cols]
        dg = dg_ref[i]
        vpart_ref[:, cols] = nn(own.astype(BF), ng)
        vglob = nn(glob.astype(BF), ng)
        d_own = jnp.where(own_mask(n, blk), nt(v_ref[:, cols], ng) + dg, 0.0).astype(BF)
        d_prev = jnp.where(
            prev_mask(reach, n, blk, pos), nt(kv_ref[reach:, cols], ng) + dg, 0.0
        ).astype(BF)
        d_glob = jnp.where(
            glob_mask(ngl, n, blk, pos, ids), nt(glob_ref[0, 0, ngl:, cols], ng) + dg, 0.0
        ).astype(BF)
        qu = (tn(d_own, kf) + tn(d_prev, kfp) + tn(d_glob, kfg)) * qf.astype(F32)
        ku = nn(d_own, qf) * kf.astype(F32)
        kup = nn(d_prev, qf) * kfp.astype(F32)
        kug = nn(d_glob, qf) * kfg.astype(F32)
        qul, kul, kupl, kugl = qu.astype(BF), ku.astype(BF), kup.astype(BF), kug.astype(BF)
        q, k, kp, kg = q_ref[:, cols], k_ref[:, cols], kv_ref[:reach, cols], glob_ref[0, 0, :ngl, cols]
        qg_ref[:, cols] = row_grad(qu, qul, q, freq, scale).astype(BF)
        kpart_ref[:, cols] = row_grad(ku, kul, k, freq, scale)
        z_ref[i, 0:m, :] = (
            scale * (tn(qul, q) + tn(kul, k) + tn(kupl, kp) + tn(kugl, kg))
        ).astype(BF)
        z_ref[i, m : m + ngl, :] = row_grad(kug, kugl, kg, freq, scale).astype(BF)
        z_ref[i, m + ngl : m + 2 * ngl, :] = vglob.astype(BF)
        z_ref[i, m + 2 * ngl :, :] = jnp.broadcast_to(gp_ref[i], (PAD, dh)).astype(BF)


def next_kernel(
    sc_ref, qn_ref, ngn_ref, k_ref, v_ref, kf_ref, f_ref, kpart_ref, vpart_ref, kg_ref, vg_ref
):
    dh = f_ref.shape[2]
    scale = dh ** (-0.25)
    reach = qn_ref.shape[0]
    n = k_ref.shape[0]
    mask = next_mask(n, reach, n // BPD, sc_ref[0], sc_ref[3])
    for i in range(HB):
        freq = f_ref[i].astype(BF)
        cols = slice(i * dh, (i + 1) * dh)
        qf = feats(qn_ref[:, cols], freq)
        kf = kf_ref[i]
        ng = ngn_ref[:reach, cols]
        tail = ngn_ref[reach:, cols].astype(F32)
        dg = jnp.concatenate([tail[0:1], tail[PAD // 2 : PAD // 2 + 1]], axis=1)[:, :reach]
        pt = jnp.where(mask, nt(kf, qf), 0.0).astype(BF)
        dt = jnp.where(mask, nt(v_ref[:, cols], ng) + dg, 0.0).astype(BF)
        vg_ref[:, cols] = vpart_ref[:, cols] + nn(pt, ng)
        ku = nn(dt, qf) * kf.astype(F32)
        kg_ref[:, cols] = kpart_ref[:, cols] + row_grad(
            ku, ku.astype(BF), k_ref[:, cols], freq, scale
        )


def add_kernel(sc_ref, kpart_ref, vpart_ref, *refs):
    z_refs, (kg_ref, vg_ref, fq_ref, gp_ref) = refs[:HB], refs[HB:]
    m, dh = fq_ref.shape[1:]
    n = kpart_ref.shape[0]
    blk = n // BPD
    pos = sc_ref[0]
    for i, z_ref in enumerate(z_refs):
        cols = slice(i * dh, (i + 1) * dh)
        fq_ref[i] = z_ref[0, 0, 0:m, :].astype(F32)
        part = [
            z_ref[0, 0, m + j * blk : m + (j + 1) * blk, :].astype(F32) for j in range(4)
        ]
        for r in range(BPD):
            here = pos * BPD + r
            w0 = jnp.where(sc_ref[1] == here, 1.0, 0.0).astype(F32)
            w1 = jnp.where(sc_ref[2] == here, 1.0, 0.0).astype(F32)
            rows = slice(r * blk, (r + 1) * blk)
            kg_ref[rows, cols] = (kpart_ref[rows, cols] + w0 * part[0] + w1 * part[1]).astype(BF)
            vg_ref[rows, cols] = (vpart_ref[rows, cols] + w0 * part[2] + w1 * part[3]).astype(BF)
        gp_ref[i] = z_ref[0, 0, m + 4 * blk : m + 4 * blk + 1, :].astype(F32)


def piece_map(paired, start, stride, offset):
    def place(h, sc):
        piece = start + h * stride + offset
        if not paired:
            return 0, piece
        return (piece // 4) ^ sc[4], (sc[5] - piece % 4 + 4) % 4

    return place


def head_call(kernel, scal, first, steps, ins, outs, args, name, flops):
    def spec(kind, array):
        shape = array.shape
        if kind == "c" or kind == "b":
            base = first if kind == "c" else 0
            wide = HB * 128
            return pl.BlockSpec((shape[0], wide), lambda h, sc: (0, h + base))
        if kind == "h" or kind == "l":
            base = first if kind == "h" else 0
            return pl.BlockSpec(
                (HB,) + shape[1:], lambda h, sc: (h + base,) + (0,) * (len(shape) - 1)
            )
        if kind == "p":
            return pl.BlockSpec((1,) + shape[1:], lambda h, sc: (h, 0, 0))
        if kind == "a":
            return pl.BlockSpec(shape, lambda h, sc: (0,) * len(shape))
        return pl.BlockSpec((1, 1) + shape[2:], lambda h, sc: kind(h, sc) + (0, 0))

    total = sum(a.size * a.dtype.itemsize for a in args) + sum(
        o.size * o.dtype.itemsize for _, o in outs
    )
    return pl.pallas_call(
        kernel,
        grid_spec=pltpu.PrefetchScalarGridSpec(
            num_scalar_prefetch=1,
            grid=(steps,),
            in_specs=[spec(kind, a) for kind, a in zip(ins, args)],
            out_specs=[spec(kind, o) for kind, o in outs],
        ),
        out_shape=[o for _, o in outs],
        name=name,
        cost_estimate=pl.CostEstimate(flops=flops, bytes_accessed=total, transcendentals=0),
    )(scal, *args)


def total_paired(array, x, z):
    pairs = [(i, i ^ 1) for i in range(8)]
    turn = {k: [(i, (i + 2 * k) % 8) for i in range(8)] for k in (1, 2, 3)}
    array = array.reshape((2, 4) + array.shape[1:])
    pick = lambda a, i: lax.dynamic_index_in_dim(a, i, 0, keepdims=False)
    half = (
        pick(array, x).astype(F32) + lax.ppermute(pick(array, 1 - x), "ctx", pairs).astype(F32)
    ).astype(BF)
    sent = [lax.ppermute(pick(half, (z + k) % 4), "ctx", turn[k]) for k in (1, 2, 3)]
    piece = (pick(half, z).astype(F32) + sum(s.astype(F32) for s in sent)).astype(BF)
    column = jnp.stack([piece] + [lax.ppermute(piece, "ctx", turn[k]) for k in (1, 2, 3)])
    other = lax.ppermute(column, "ctx", pairs)
    return jnp.stack([column, other])


def total_exchanged(array, count):
    shape = array.shape
    flat = array.reshape(count, -1, shape[-1])
    parts = lax.all_to_all(flat, "ctx", 0, 0, tiled=True)
    piece = jnp.sum(parts.astype(F32), axis=0).astype(BF)
    parts = lax.all_to_all(
        jnp.broadcast_to(piece[None], (count,) + piece.shape), "ctx", 0, 0, tiled=True
    )
    return parts.reshape((1,) + shape)


def local(query_rows, key_rows, value_rows, frequencies, norm_gain, out_grad, global_ids):
    count = lax.axis_size("ctx")
    pos = lax.axis_index("ctx").astype(jnp.int32)
    n, width = query_rows.shape
    heads, m, dh = frequencies.shape
    blk = n // BPD
    reach = (WIN - 1) * blk
    steps = heads // HB
    paired = count == 8 and heads == 16
    x, z = pos % 2, pos // 2
    sds = jax.ShapeDtypeStruct
    unit = 2 * n * m * dh
    ids = global_ids.astype(jnp.int32)
    scal = jnp.stack([pos, ids[0], ids[1], jnp.int32(count - 1), x, z])
    gain = norm_gain.reshape(1, width)
    forth = [(i, i + 1) for i in range(count - 1)]
    back = [(i + 1, i) for i in range(count - 1)]
    total = (lambda a: total_paired(a, x, z)) if paired else (lambda a: total_exchanged(a, count))

    kv, glob = head_call(
        gather_kernel, scal, 0, steps, "cc",
        [("c", sds((2 * reach, width), BF)), ("p", sds((steps, 4 * blk, HB * dh), BF))],
        (key_rows, value_rows), "gather", unit,
    )
    glob = total(glob)
    kv = lax.ppermute(kv, "ctx", forth)
    qn = lax.ppermute(query_rows[:reach], "ctx", back)

    qf, kf = head_call(
        feat_kernel, scal, 0, steps, "cch",
        [("h", sds((heads, n, m), BF)), ("h", sds((heads, n, m), BF))],
        (query_rows, key_rows, frequencies), "features", 2 * heads * unit,
    )
    gmap = piece_map(paired, 0, 1, 0)
    att, kfp, kfg, rows, sums = head_call(
        forward_kernel, scal, 0, steps, ["h", "h", "c", gmap, "c", "h", "c", "c"],
        [
            ("h", sds((heads, dh, n), F32)),
            ("h", sds((heads, reach, m), BF)),
            ("h", sds((heads, 2 * blk, m), BF)),
            ("h", sds((heads, 8, n), F32)),
            ("a", sds((2, n), F32)),
        ],
        (qf, kf, kv, glob, value_rows, frequencies, out_grad, gain),
        "forward", 6 * heads * unit,
    )
    sums = lax.psum(sums, "head")
    ng, ngs, dg, gp = head_call(
        norm_kernel, scal, 0, steps, "ahhcc",
        [
            ("c", sds((n, width), BF)),
            ("c", sds((reach + PAD, width), BF)),
            ("h", sds((heads, 1, n), F32)),
            ("h", sds((heads, 1, dh), F32)),
        ],
        (sums, rows, att, out_grad, gain), "norm", heads * unit // 16,
    )
    ngn = lax.ppermute(ngs, "ctx", back)
    zrows = m + 4 * blk + PAD
    chunks = 2 if paired else 1
    per = steps // chunks
    parts, gathered = [], []
    for c in range(chunks):
        gmap = piece_map(paired, c * per, 1, 0)
        qg, kpart, vpart, zc = head_call(
            backward_kernel, scal, c * per, per,
            ["c", "c", "c", gmap, "c", "h", "h", "h", "h", "c", "h", "h", "h"],
            [
                ("b", sds((n, width // chunks), BF)),
                ("b", sds((n, width // chunks), F32)),
                ("b", sds((n, width // chunks), F32)),
                ("l", sds((heads // chunks, zrows, dh), BF)),
            ],
            (query_rows, key_rows, kv, glob, value_rows, qf, kf, kfp, kfg, ng, dg, gp, frequencies),
            "backward", 16 * heads * unit // chunks,
        )
        parts.append((qg, kpart, vpart))
        gathered.append(total(zc))
    qg, kpart, vpart = (jnp.concatenate(p, axis=1) for p in zip(*parts))
    kpart, vpart = head_call(
        next_kernel, scal, 0, steps, "cccchhcc",
        [("c", sds((n, width), F32)), ("c", sds((n, width), F32))],
        (qn, ngn, key_rows, value_rows, kf, frequencies, kpart, vpart),
        "following", 5 * heads * unit,
    )
    outs = []
    for c in range(chunks):
        zmaps = [piece_map(paired, 0, HB, i) for i in range(HB)]
        outs.append(
            head_call(
                add_kernel, scal, c * per, per, ["c", "c"] + zmaps,
                [
                    ("b", sds((n, width // chunks), BF)),
                    ("b", sds((n, width // chunks), BF)),
                    ("l", sds((heads // chunks, m, dh), F32)),
                    ("l", sds((heads // chunks, 1, dh), F32)),
                ],
                (kpart, vpart) + (gathered[c],) * HB, "finish", heads * unit // 64,
            )
        )
    kgrad, vgrad = (jnp.concatenate(p, axis=1) for p in list(zip(*outs))[:2])
    fgrad, gain_grad = (jnp.concatenate(p, axis=0) for p in list(zip(*outs))[2:])
    return (qg, kgrad, vgrad, fgrad, gain_grad.reshape(-1))


def solution(mesh):
    strips = P("ctx", "head")
    return jax.shard_map(
        local,
        mesh=mesh,
        in_specs=(strips, strips, strips, P("head", None, None), P("head"), strips, P()),
        out_specs=(strips, strips, strips, P("head", None, None), P("head")),
        check_vma=False,
    )
```

```python
import jax
import jax.numpy as jnp
from jax import lax
from jax.experimental import pallas as pl
from jax.experimental.pallas import tpu as pltpu
from jax.sharding import PartitionSpec as P


D = 8192
BPD = 4
WIN = 4
EPS = 1e-05
BF = jnp.bfloat16
F32 = jnp.float32
PAD = 16


def nt(a, b):
    return lax.dot_general(a, b, (((1,), (1,)), ((), ())), preferred_element_type=F32)


def nn(a, b):
    return lax.dot_general(a, b, (((1,), (0,)), ((), ())), preferred_element_type=F32)


def tn(a, b):
    return lax.dot_general(a, b, (((0,), (0,)), ((), ())), preferred_element_type=F32)


def feats(rows, freq):
    scale = rows.shape[-1] ** (-0.25)
    wide = rows.astype(F32)
    square = jnp.sum(wide * wide, axis=-1, keepdims=True)
    score = nt(rows, freq)
    return (
        jnp.exp(scale * score - (0.5 * scale * scale) * square) * freq.shape[0] ** (-0.5)
    ).astype(BF)


def block_of(shape, axis, length):
    return lax.broadcasted_iota(jnp.int32, shape, axis) // length


def keep(mask):
    return jnp.where(mask, 1.0, 0.0).astype(F32)


def fill_masks(sc_ref, own_ref, ext_ref):
    n = own_ref.shape[0]
    blk = n // BPD
    reach = (WIN - 1) * blk
    pos = sc_ref[0]
    own_ref[...] = keep(block_of((n, n), 0, blk) <= block_of((n, n), 1, blk))
    before = block_of((reach, n), 0, blk) >= block_of((reach, n), 1, blk)
    ext_ref[:reach, :] = keep(before & (pos > 0))
    shape = (2 * blk, n)
    target = jnp.where(block_of(shape, 0, blk) == 0, sc_ref[1], sc_ref[2])
    query = block_of(shape, 1, blk) + pos * BPD
    ext_ref[reach:, :] = keep((target > query) | (target <= query - WIN))


def masked(values, mask):
    return jnp.where(mask > 0.5, values, 0.0)


def over(count, body, unroll=1):
    def step(i, carry):
        for j in range(unroll):
            body(i * unroll + j)
        return carry

    lax.fori_loop(0, count // unroll, step, 0)


def lanes(h, dh):
    return pl.ds(pl.multiple_of(h * dh, dh), dh)


def gather_kernel(sc_ref, k_ref, v_ref, glob_ref):
    n = k_ref.shape[0]
    blk = n // BPD
    pieces, _, wide = glob_ref.shape
    pos = sc_ref[0]
    for g in range(2):
        at = sc_ref[1 + g] - pos * BPD
        here = (at >= 0) & (at < BPD)
        start = pl.multiple_of(jnp.clip(at, 0, BPD - 1) * blk, blk)
        for i, src in enumerate((k_ref, v_ref)):
            first = (2 * i + g) * blk
            for p in range(pieces):
                rows = src[pl.ds(start, blk), p * wide : (p + 1) * wide]
                glob_ref[p, first : first + blk, :] = jnp.where(here, rows, jnp.zeros_like(rows))


def feat_kernel(q_ref, k_ref, f_ref, qf_ref, kf_ref):
    heads, _, dh = f_ref.shape

    def body(h):
        freq = f_ref[h].astype(BF)
        qf_ref[h] = feats(q_ref[:, lanes(h, dh)], freq)
        kf_ref[h] = feats(k_ref[:, lanes(h, dh)], freq)

    over(heads, body, 2)


def forward_kernel(
    sc_ref, qf_ref, kf_ref, kp_ref, vp_ref, glob_ref, v_ref, f_ref, g_ref, gain_ref,
    att_ref, kfe_ref, rows_ref, sums_ref, own_ref, ext_ref,
):
    heads, _, dh = f_ref.shape
    reach = kp_ref.shape[0]
    half = glob_ref.shape[1] // 2
    fill_masks(sc_ref, own_ref, ext_ref)
    sums_ref[...] = jnp.zeros_like(sums_ref)

    def head(h, piece, j):
        freq = f_ref[h].astype(BF)
        cols = lanes(h, dh)
        side = slice(j * dh, (j + 1) * dh)
        kfe_ref[h, :reach, :] = feats(kp_ref[:, cols], freq)
        kfe_ref[h, reach:, :] = feats(glob_ref[piece, :half, side], freq)
        qf = qf_ref[h]
        own = masked(nt(kf_ref[h], qf), own_ref[...])
        ext = masked(nt(kfe_ref[h], qf), ext_ref[...])
        den = jnp.sum(own, axis=0, keepdims=True) + jnp.sum(ext, axis=0, keepdims=True)
        ext = ext.astype(BF)
        num = (
            tn(v_ref[:, cols], own.astype(BF))
            + tn(vp_ref[:, cols], ext[:reach])
            + tn(glob_ref[piece, half:, side], ext[reach:])
        )
        att = num / den
        gg = (gain_ref[:, cols] * g_ref[:, cols].astype(F32)).T
        square = jnp.sum(att * att, axis=0, keepdims=True)
        product = jnp.sum(att * gg, axis=0, keepdims=True)
        att_ref[h] = att
        rows_ref[h, 0:1, :] = den
        rows_ref[h, 1:2, :] = square
        rows_ref[h, 2:3, :] = product
        sums_ref[0:1, :] += square
        sums_ref[1:2, :] += product

    def body(p):
        head(2 * p, p, 0)
        head(2 * p + 1, p, 1)

    over(heads // 2, body)


def norm_kernel(
    sums_ref, rows_ref, att_ref, g_ref, gain_ref, ng_ref, ngs_ref, dg_ref, gp_ref
):
    heads, dh, _ = att_ref.shape
    alpha = lax.rsqrt(sums_ref[0:1, :] / D + EPS)
    beta = alpha * alpha * alpha * sums_ref[1:2, :] / D
    reach = ngs_ref.shape[0] - PAD

    def body(h):
        cols = lanes(h, dh)
        den = rows_ref[h, 0:1, :]
        att = att_ref[h]
        wide = g_ref[:, cols].astype(F32)
        gg = (gain_ref[:, cols] * wide).T
        ng = ((alpha * gg - att * beta) / den).T.astype(BF)
        dg = -(alpha * rows_ref[h, 2:3, :] - beta * rows_ref[h, 1:2, :]) / den
        ng_ref[:, cols] = ng
        dg_ref[h] = dg
        ngs_ref[:reach, cols] = ng[:reach]
        pieces = [jnp.broadcast_to(dg[:, j : j + dh], (PAD // 2, dh)) for j in (0, dh)]
        ngs_ref[reach:, cols] = jnp.concatenate(pieces, axis=0).astype(BF)
        gp_ref[h] = jnp.sum(wide * (att * alpha).T, axis=0, keepdims=True)

    over(heads, body, 2)


def row_grad(u, low, rows, freq, scale):
    return scale * nn(low, freq) - (scale * scale) * rows.astype(F32) * jnp.sum(
        u, axis=-1, keepdims=True
    )


def backward_kernel(first):
    def kernel(
        sc_ref, q_ref, k_ref, kp_ref, vp_ref, glob_ref, v_ref, qf_ref, kf_ref, kfe_ref,
        ng_ref, dg_ref, gp_ref, f_ref,
        qg_ref, kpart_ref, vpart_ref, z_ref, own_ref, ext_ref,
    ):
        _, m, dh = f_ref.shape
        scale = dh ** (-0.25)
        reach = kp_ref.shape[0]
        ngl = glob_ref.shape[1] // 2
        fill_masks(sc_ref, own_ref, ext_ref)

        def head(i, h, piece, j):
            freq = f_ref[h].astype(BF)
            cols = lanes(h, dh)
            outs = lanes(i, dh)
            side = slice(j * dh, (j + 1) * dh)
            qf, kf, kfe = qf_ref[h], kf_ref[h], kfe_ref[h]
            ng = ng_ref[:, cols]
            dg = dg_ref[h]
            own = masked(nt(kf, qf), own_ref[...]).astype(BF)
            vpart_ref[:, outs] = nn(own, ng)
            glob = masked(nt(kfe[reach:], qf), ext_ref[reach:, :]).astype(BF)
            z_ref[i, m + ngl : m + 2 * ngl, :] = nn(glob, ng).astype(BF)
            d_own = masked(nt(v_ref[:, cols], ng) + dg, own_ref[...]).astype(BF)
            d_prev = masked(nt(vp_ref[:, cols], ng) + dg, ext_ref[:reach, :]).astype(BF)
            d_glob = masked(
                nt(glob_ref[piece, ngl:, side], ng) + dg, ext_ref[reach:, :]
            ).astype(BF)
            d_ext = jnp.concatenate([d_prev, d_glob], axis=0)
            qu = (tn(d_own, kf) + tn(d_ext, kfe)) * qf.astype(F32)
            ku = nn(d_own, qf) * kf.astype(F32)
            kue = nn(d_ext, qf) * kfe.astype(F32)
            qul, kul, kuel = qu.astype(BF), ku.astype(BF), kue.astype(BF)
            q, k, kp, kg = q_ref[:, cols], k_ref[:, cols], kp_ref[:, cols], glob_ref[piece, :ngl, side]
            qg_ref[:, outs] = row_grad(qu, qul, q, freq, scale).astype(BF)
            kpart_ref[:, outs] = row_grad(ku, kul, k, freq, scale)
            z_ref[i, 0:m, :] = (
                scale * (tn(qul, q) + tn(kul, k) + tn(kuel[:reach], kp) + tn(kuel[reach:], kg))
            ).astype(BF)
            z_ref[i, m : m + ngl, :] = row_grad(kue[reach:], kuel[reach:], kg, freq, scale).astype(BF)
            z_ref[i, m + 2 * ngl :, :] = jnp.broadcast_to(gp_ref[h], (PAD, dh)).astype(BF)

        def body(p):
            head(2 * p, 2 * p + first, p + first // 2, 0)
            head(2 * p + 1, 2 * p + 1 + first, p + first // 2, 1)

        over(z_ref.shape[0] // 2, body)

    return kernel


def next_kernel(sc_ref, qn_ref, ngn_ref, k_ref, v_ref, kf_ref, f_ref, *refs):
    chunks = (len(refs) - 4) // 3
    parts, (qg_ref, kg_ref, vg_ref, mask_ref) = refs[: 3 * chunks], refs[3 * chunks :]
    heads, _, dh = f_ref.shape
    scale = dh ** (-0.25)
    reach = qn_ref.shape[0]
    n = k_ref.shape[0]
    blk = n // BPD
    after = block_of((n, reach), 0, blk) >= block_of((n, reach), 1, blk) + 1
    mask_ref[...] = keep(after & (sc_ref[0] < sc_ref[3]))
    per = heads // chunks

    def head(i, c):
        qg_in, kpart_ref, vpart_ref = parts[3 * c : 3 * c + 3]
        h = i + c * per
        freq = f_ref[h].astype(BF)
        cols = lanes(h, dh)
        ins = lanes(i, dh)
        qf = feats(qn_ref[:, cols], freq)
        kf = kf_ref[h]
        ng = ngn_ref[:reach, cols]
        tail = ngn_ref[reach:, cols].astype(F32)
        dg = jnp.concatenate([tail[0:1], tail[PAD // 2 : PAD // 2 + 1]], axis=1)[:, :reach]
        pt = masked(nt(kf, qf), mask_ref[...]).astype(BF)
        dt = masked(nt(v_ref[:, cols], ng) + dg, mask_ref[...]).astype(BF)
        vg_ref[:, cols] = vpart_ref[:, ins] + nn(pt, ng)
        ku = nn(dt, qf) * kf.astype(F32)
        kg_ref[:, cols] = kpart_ref[:, ins] + row_grad(
            ku, ku.astype(BF), k_ref[:, cols], freq, scale
        )
        qg_ref[:, cols] = qg_in[:, ins]

    def body(i):
        for c in range(chunks):
            head(i, c)

    over(per, body)


def add_kernel(sc_ref, kpart_ref, vpart_ref, *refs):
    z_refs, (kg_ref, vg_ref, fq_ref, gp_ref) = refs[:-4], refs[-4:]
    heads, m, dh = fq_ref.shape
    n = kpart_ref.shape[0]
    blk = n // BPD
    pos = sc_ref[0]
    weights = [
        [jnp.where(sc_ref[1 + g] == pos * BPD + r, 1.0, 0.0).astype(F32) for g in range(2)]
        for r in range(BPD)
    ]

    def finish(h, tile):
        cols = lanes(h, dh)
        fq_ref[h] = tile(slice(0, m))
        part = [tile(slice(m + j * blk, m + (j + 1) * blk)) for j in range(4)]
        for r in range(BPD):
            w0, w1 = weights[r]
            rows = slice(r * blk, (r + 1) * blk)
            kg_ref[rows, cols] = (kpart_ref[rows, cols] + w0 * part[0] + w1 * part[1]).astype(BF)
            vg_ref[rows, cols] = (vpart_ref[rows, cols] + w0 * part[2] + w1 * part[3]).astype(BF)
        gp_ref[h] = tile(slice(m + 4 * blk, m + 4 * blk + 1))

    if len(z_refs) == 1:
        over(heads, lambda h: finish(h, lambda rows: z_refs[0][0, h, rows, :].astype(F32)))
        return
    chunks = len(z_refs) // 2

    def body(i):
        mine = (i // 4) == sc_ref[4]
        slot = lax.rem(sc_ref[5] - lax.rem(i, 4) + 4, 4)
        for c in range(chunks):
            near, far = z_refs[2 * c : 2 * c + 2]
            finish(
                i + c * (heads // chunks),
                lambda rows: jnp.where(mine, near[slot, rows, :], far[slot, rows, :]).astype(F32),
            )

    over(heads // chunks, body)


def call(kernel, ins, outs, args, flops, scratch=()):
    place = {
        "s": pl.BlockSpec(memory_space=pltpu.SMEM),
        "v": pl.BlockSpec(memory_space=pltpu.VMEM),
    }
    total = sum(a.size * a.dtype.itemsize for a in args) + sum(
        o.size * o.dtype.itemsize for o in outs
    )
    return pl.pallas_call(
        kernel,
        in_specs=[place[kind] for kind in ins],
        out_specs=[place["v"] for _ in outs],
        out_shape=list(outs),
        scratch_shapes=list(scratch),
        compiler_params=pltpu.CompilerParams(vmem_limit_bytes=16 * 1024 * 1024),
        cost_estimate=pl.CostEstimate(flops=flops, bytes_accessed=total, transcendentals=0),
    )(*args)


def total_paired(array, x, z):
    pairs = [(i, i ^ 1) for i in range(8)]
    turn = {k: [(i, (i + 2 * k) % 8) for i in range(8)] for k in (1, 2, 3)}
    array = array.reshape((2, 4) + array.shape[1:])
    pick = lambda a, i: lax.dynamic_index_in_dim(a, i, 0, keepdims=False)
    got = lax.ppermute(pick(array, 1 - x), "ctx", pairs)
    half = (pick(array, x).astype(F32) + got.astype(F32)).astype(BF)
    sent = []
    for k in (2, 1, 3):
        sent.append(lax.ppermute(pick(half, (z + k) % 4), "ctx", turn[k]))
    piece = (pick(half, z).astype(F32) + sum(s.astype(F32) for s in sent)).astype(BF)
    column = [piece]
    for k in (1, 2, 3):
        column.append(lax.ppermute(piece, "ctx", turn[k]))
    column = jnp.stack(column)
    other = lax.ppermute(column, "ctx", pairs)
    return column, other


def total_exchanged(array, count):
    shape = array.shape
    flat = array.reshape(count, -1, shape[-1])
    parts = lax.all_to_all(flat, "ctx", 0, 0, tiled=True)
    piece = jnp.sum(parts.astype(F32), axis=0).astype(BF)
    wide = jnp.broadcast_to(piece[None], (count,) + piece.shape)
    parts = lax.all_to_all(wide, "ctx", 0, 0, tiled=True)
    return parts.reshape(shape)


def local(query_rows, key_rows, value_rows, frequencies, norm_gain, out_grad, global_ids):
    count = lax.axis_size("ctx")
    pos = lax.axis_index("ctx").astype(jnp.int32)
    n, width = query_rows.shape
    heads, m, dh = frequencies.shape
    blk = n // BPD
    reach = (WIN - 1) * blk
    paired = count == 8 and heads == 16
    x, z = pos % 2, pos // 2
    sds = jax.ShapeDtypeStruct
    unit = 2 * n * m * dh * heads
    ids = global_ids.astype(jnp.int32)
    scal = jnp.stack([pos, ids[0], ids[1], jnp.int32(count - 1), x, z])
    gain = norm_gain.reshape(1, width)
    forth = [(i, i + 1) for i in range(count - 1)]
    back = [(i + 1, i) for i in range(count - 1)]
    masks = [pltpu.VMEM((n, n), F32), pltpu.VMEM((reach + 2 * blk, n), F32)]

    (glob,) = call(
        gather_kernel, "svv", [sds((heads // 2, 4 * blk, 2 * dh), BF)],
        (scal, key_rows, value_rows), unit // 16,
    )
    glob = total_exchanged(glob, count)
    kp = lax.ppermute(key_rows[n - reach :], "ctx", forth)
    vp = lax.ppermute(value_rows[n - reach :], "ctx", forth)
    qn = lax.ppermute(query_rows[:reach], "ctx", back)

    qf, kf = call(
        feat_kernel, "vvv", [sds((heads, n, m), BF), sds((heads, n, m), BF)],
        (query_rows, key_rows, frequencies), 2 * unit,
    )
    att, kfe, rows, sums = call(
        forward_kernel, "svvvvvvvvv",
        [
            sds((heads, dh, n), F32),
            sds((heads, reach + 2 * blk, m), BF),
            sds((heads, 8, n), F32),
            sds((2, n), F32),
        ],
        (scal, qf, kf, kp, vp, glob, value_rows, frequencies, out_grad, gain),
        6 * unit, masks,
    )
    sums = lax.psum(sums, "head")
    ng, ngs, dg, gp = call(
        norm_kernel, "vvvvv",
        [
            sds((n, width), BF),
            sds((reach + PAD, width), BF),
            sds((heads, 1, n), F32),
            sds((heads, 1, dh), F32),
        ],
        (sums, rows, att, out_grad, gain), unit // 16,
    )
    ngn = lax.ppermute(ngs, "ctx", back)
    zrows = m + 4 * blk + PAD
    chunks = 2 if paired else 1
    per = heads // chunks
    parts, gathered = [], []
    for c in range(chunks):
        *part, zc = call(
            backward_kernel(c * per), "s" + "v" * 13,
            [
                sds((n, per * dh), BF),
                sds((n, per * dh), F32),
                sds((n, per * dh), F32),
                sds((per, zrows, dh), BF),
            ],
            (scal, query_rows, key_rows, kp, vp, glob, value_rows, qf, kf, kfe, ng, dg, gp,
             frequencies),
            16 * unit // chunks, masks,
        )
        parts += part
        if paired:
            gathered += total_paired(zc, x, z)
        else:
            gathered.append(total_exchanged(zc, count)[None])
    qg, kpart, vpart = call(
        next_kernel, "s" + "v" * (6 + 3 * chunks),
        [sds((n, width), BF), sds((n, width), F32), sds((n, width), F32)],
        (scal, qn, ngn, key_rows, value_rows, kf, frequencies, *parts),
        5 * unit, [pltpu.VMEM((n, reach), F32)],
    )
    kgrad, vgrad, fgrad, gain_grad = call(
        add_kernel, "s" + "v" * (2 + len(gathered)),
        [
            sds((n, width), BF),
            sds((n, width), BF),
            sds((heads, m, dh), F32),
            sds((heads, 1, dh), F32),
        ],
        (scal, kpart, vpart, *gathered), unit // 64,
    )
    return (qg, kgrad, vgrad, fgrad, gain_grad.reshape(-1))


def solution(mesh):
    strips = P("ctx", "head")

    return jax.shard_map(
        local,
        mesh=mesh,
        in_specs=(strips, strips, strips, P("head", None, None), P("head"), strips, P()),
        out_specs=(strips, strips, strips, P("head", None, None), P("head")),
        check_vma=False,
    )
```

```python
import jax
import jax.numpy as jnp
from jax import lax
from jax.experimental import pallas as pl
from jax.experimental.pallas import tpu as pltpu
from jax.sharding import PartitionSpec as P


D = 8192
BPD = 4
WIN = 4
EPS = 1e-05
BF = jnp.bfloat16
F32 = jnp.float32
HB = 2
PAD = 16


def nt(a, b):
    return lax.dot_general(a, b, (((1,), (1,)), ((), ())), preferred_element_type=F32)


def nn(a, b):
    return lax.dot_general(a, b, (((1,), (0,)), ((), ())), preferred_element_type=F32)


def tn(a, b):
    return lax.dot_general(a, b, (((0,), (0,)), ((), ())), preferred_element_type=F32)


def feats(rows, freq):
    scale = rows.shape[-1] ** (-0.25)
    wide = rows.astype(F32)
    square = jnp.sum(wide * wide, axis=-1, keepdims=True)
    score = nt(rows, freq)
    return (
        jnp.exp(scale * score - (0.5 * scale * scale) * square) * freq.shape[0] ** (-0.5)
    ).astype(BF)


def block_of(shape, axis, length):
    return lax.broadcasted_iota(jnp.int32, shape, axis) // length


def keep(mask):
    return jnp.where(mask, 1.0, 0.0).astype(F32)


def fill_masks(sc_ref, own_ref, ext_ref):
    n = own_ref.shape[0]
    blk = n // BPD
    reach = (WIN - 1) * blk
    pos = sc_ref[0]
    own_ref[...] = keep(block_of((n, n), 0, blk) <= block_of((n, n), 1, blk))
    before = block_of((reach, n), 0, blk) >= block_of((reach, n), 1, blk)
    ext_ref[:reach, :] = keep(before & (pos > 0))
    shape = (2 * blk, n)
    target = jnp.where(block_of(shape, 0, blk) == 0, sc_ref[1], sc_ref[2])
    query = block_of(shape, 1, blk) + pos * BPD
    ext_ref[reach:, :] = keep((target > query) | (target <= query - WIN))


def masked(values, mask):
    return jnp.where(mask > 0.5, values, 0.0)


def over(count, body, unroll=1):
    def step(i, carry):
        for j in range(unroll):
            body(i * unroll + j)
        return carry

    lax.fori_loop(0, count // unroll, step, 0)


def lanes(h, dh):
    return pl.ds(pl.multiple_of(h * dh, dh), dh)


def gather_kernel(sc_ref, k_ref, v_ref, glob_ref):
    n = k_ref.shape[0]
    blk = n // BPD
    pieces, _, wide = glob_ref.shape
    pos = sc_ref[0]
    for g in range(2):
        at = sc_ref[1 + g] - pos * BPD
        here = (at >= 0) & (at < BPD)
        start = pl.multiple_of(jnp.clip(at, 0, BPD - 1) * blk, blk)
        for i, src in enumerate((k_ref, v_ref)):
            first = (2 * i + g) * blk
            for p in range(pieces):
                rows = src[pl.ds(start, blk), p * wide : (p + 1) * wide]
                glob_ref[p, first : first + blk, :] = jnp.where(here, rows, jnp.zeros_like(rows))


def feat_kernel(q_ref, k_ref, f_ref, qf_ref, kf_ref):
    heads, _, dh = f_ref.shape

    def body(h):
        freq = f_ref[h].astype(BF)
        qf_ref[h] = feats(q_ref[:, lanes(h, dh)], freq)
        kf_ref[h] = feats(k_ref[:, lanes(h, dh)], freq)

    over(heads, body, 2)


def forward_kernel(
    sc_ref, qf_ref, kf_ref, kp_ref, vp_ref, glob_ref, v_ref, f_ref, g_ref, gain_ref,
    att_ref, kfe_ref, rows_ref, sums_ref, own_ref, ext_ref,
):
    dh = f_ref.shape[2]
    reach = kp_ref.shape[0]
    half = glob_ref.shape[1] // 2

    @pl.when(pl.program_id(0) == 0)
    def _():
        fill_masks(sc_ref, own_ref, ext_ref)
        sums_ref[...] = jnp.zeros_like(sums_ref)

    for i in range(HB):
        freq = f_ref[i].astype(BF)
        cols = slice(i * dh, (i + 1) * dh)
        kfe_ref[i, :reach, :] = feats(kp_ref[:, cols], freq)
        kfe_ref[i, reach:, :] = feats(glob_ref[0, :half, cols], freq)
        qf = qf_ref[i]
        own = masked(nt(kf_ref[i], qf), own_ref[...])
        ext = masked(nt(kfe_ref[i], qf), ext_ref[...])
        den = jnp.sum(own, axis=0, keepdims=True) + jnp.sum(ext, axis=0, keepdims=True)
        ext = ext.astype(BF)
        num = (
            tn(v_ref[:, cols], own.astype(BF))
            + tn(vp_ref[:, cols], ext[:reach])
            + tn(glob_ref[0, half:, cols], ext[reach:])
        )
        att = num / den
        gg = (gain_ref[:, cols] * g_ref[:, cols].astype(F32)).T
        square = jnp.sum(att * att, axis=0, keepdims=True)
        product = jnp.sum(att * gg, axis=0, keepdims=True)
        att_ref[i] = att
        rows_ref[i, 0:1, :] = den
        rows_ref[i, 1:2, :] = square
        rows_ref[i, 2:3, :] = product
        rows_ref[i, 3:8, :] = jnp.zeros((5, den.shape[1]), F32)
        sums_ref[0:1, :] += square
        sums_ref[1:2, :] += product


def norm_kernel(
    sums_ref, rows_ref, att_ref, g_ref, gain_ref, ng_ref, ngs_ref, dg_ref, gp_ref
):
    heads, dh, _ = att_ref.shape
    alpha = lax.rsqrt(sums_ref[0:1, :] / D + EPS)
    beta = alpha * alpha * alpha * sums_ref[1:2, :] / D
    reach = ngs_ref.shape[0] - PAD

    def body(h):
        cols = lanes(h, dh)
        den = rows_ref[h, 0:1, :]
        att = att_ref[h]
        wide = g_ref[:, cols].astype(F32)
        gg = (gain_ref[:, cols] * wide).T
        ng = ((alpha * gg - att * beta) / den).T.astype(BF)
        dg = -(alpha * rows_ref[h, 2:3, :] - beta * rows_ref[h, 1:2, :]) / den
        ng_ref[:, cols] = ng
        dg_ref[h] = dg
        ngs_ref[:reach, cols] = ng[:reach]
        pieces = [jnp.broadcast_to(dg[:, j : j + dh], (PAD // 2, dh)) for j in (0, dh)]
        ngs_ref[reach:, cols] = jnp.concatenate(pieces, axis=0).astype(BF)
        gp_ref[h] = jnp.sum(wide * (att * alpha).T, axis=0, keepdims=True)

    over(heads, body, 2)


def row_grad(u, low, rows, freq, scale):
    return scale * nn(low, freq) - (scale * scale) * rows.astype(F32) * jnp.sum(
        u, axis=-1, keepdims=True
    )


def backward_kernel(
    sc_ref, q_ref, k_ref, kp_ref, vp_ref, glob_ref, v_ref, qf_ref, kf_ref, kfe_ref,
    ng_ref, dg_ref, gp_ref, f_ref,
    qg_ref, kpart_ref, vpart_ref, z_ref, own_ref, ext_ref,
):
    _, m, dh = f_ref.shape
    scale = dh ** (-0.25)
    reach = kp_ref.shape[0]
    ngl = glob_ref.shape[1] // 2

    @pl.when(pl.program_id(0) == 0)
    def _():
        fill_masks(sc_ref, own_ref, ext_ref)

    for i in range(HB):
        freq = f_ref[i].astype(BF)
        cols = slice(i * dh, (i + 1) * dh)
        qf, kf, kfe = qf_ref[i], kf_ref[i], kfe_ref[i]
        ng = ng_ref[:, cols]
        dg = dg_ref[i]
        own = masked(nt(kf, qf), own_ref[...]).astype(BF)
        vpart_ref[:, cols] = nn(own, ng)
        glob = masked(nt(kfe[reach:], qf), ext_ref[reach:, :]).astype(BF)
        z_ref[i, m + ngl : m + 2 * ngl, :] = nn(glob, ng).astype(BF)
        d_own = masked(nt(v_ref[:, cols], ng) + dg, own_ref[...]).astype(BF)
        d_prev = masked(nt(vp_ref[:, cols], ng) + dg, ext_ref[:reach, :]).astype(BF)
        d_glob = masked(nt(glob_ref[0, ngl:, cols], ng) + dg, ext_ref[reach:, :]).astype(BF)
        d_ext = jnp.concatenate([d_prev, d_glob], axis=0)
        qu = (tn(d_own, kf) + tn(d_ext, kfe)) * qf.astype(F32)
        ku = nn(d_own, qf) * kf.astype(F32)
        kue = nn(d_ext, qf) * kfe.astype(F32)
        qul, kul, kuel = qu.astype(BF), ku.astype(BF), kue.astype(BF)
        q, k, kp, kg = q_ref[:, cols], k_ref[:, cols], kp_ref[:, cols], glob_ref[0, :ngl, cols]
        qg_ref[:, cols] = row_grad(qu, qul, q, freq, scale).astype(BF)
        kpart_ref[:, cols] = row_grad(ku, kul, k, freq, scale)
        z_ref[i, 0:m, :] = (
            scale * (tn(qul, q) + tn(kul, k) + tn(kuel[:reach], kp) + tn(kuel[reach:], kg))
        ).astype(BF)
        z_ref[i, m : m + ngl, :] = row_grad(kue[reach:], kuel[reach:], kg, freq, scale).astype(BF)
        z_ref[i, m + 2 * ngl :, :] = jnp.broadcast_to(gp_ref[i], (PAD, dh)).astype(BF)


def next_kernel(
    sc_ref, qn_ref, ngn_ref, k_ref, v_ref, kf_ref, f_ref, kpart_ref, vpart_ref,
    kg_ref, vg_ref, mask_ref,
):
    dh = f_ref.shape[2]
    scale = dh ** (-0.25)
    reach = qn_ref.shape[0]
    n = k_ref.shape[0]
    blk = n // BPD

    @pl.when(pl.program_id(0) == 0)
    def _():
        after = block_of((n, reach), 0, blk) >= block_of((n, reach), 1, blk) + 1
        mask_ref[...] = keep(after & (sc_ref[0] < sc_ref[3]))

    for i in range(HB):
        freq = f_ref[i].astype(BF)
        cols = slice(i * dh, (i + 1) * dh)
        qf = feats(qn_ref[:, cols], freq)
        kf = kf_ref[i]
        ng = ngn_ref[:reach, cols]
        tail = ngn_ref[reach:, cols].astype(F32)
        dg = jnp.concatenate([tail[0:1], tail[PAD // 2 : PAD // 2 + 1]], axis=1)[:, :reach]
        pt = masked(nt(kf, qf), mask_ref[...]).astype(BF)
        dt = masked(nt(v_ref[:, cols], ng) + dg, mask_ref[...]).astype(BF)
        vg_ref[:, cols] = vpart_ref[:, cols] + nn(pt, ng)
        ku = nn(dt, qf) * kf.astype(F32)
        kg_ref[:, cols] = kpart_ref[:, cols] + row_grad(
            ku, ku.astype(BF), k_ref[:, cols], freq, scale
        )


def add_kernel(sc_ref, kpart_ref, vpart_ref, *refs):
    z_refs, (kg_ref, vg_ref, fq_ref, gp_ref) = refs[:-4], refs[-4:]
    heads, m, dh = fq_ref.shape
    n = kpart_ref.shape[0]
    blk = n // BPD
    pos = sc_ref[0]
    weights = [
        [jnp.where(sc_ref[1 + g] == pos * BPD + r, 1.0, 0.0).astype(F32) for g in range(2)]
        for r in range(BPD)
    ]

    def finish(h, tile):
        cols = lanes(h, dh)
        fq_ref[h] = tile(slice(0, m))
        part = [tile(slice(m + j * blk, m + (j + 1) * blk)) for j in range(4)]
        for r in range(BPD):
            w0, w1 = weights[r]
            rows = slice(r * blk, (r + 1) * blk)
            kg_ref[rows, cols] = (kpart_ref[rows, cols] + w0 * part[0] + w1 * part[1]).astype(BF)
            vg_ref[rows, cols] = (vpart_ref[rows, cols] + w0 * part[2] + w1 * part[3]).astype(BF)
        gp_ref[h] = tile(slice(m + 4 * blk, m + 4 * blk + 1))

    if len(z_refs) == 1:
        over(heads, lambda h: finish(h, lambda rows: z_refs[0][0, h, rows, :].astype(F32)))
        return
    chunks = len(z_refs) // 2

    def body(i):
        mine = (i // 4) == sc_ref[4]
        slot = lax.rem(i, 4)
        for c in range(chunks):
            near, far = z_refs[2 * c : 2 * c + 2]
            finish(
                i + c * (heads // chunks),
                lambda rows: jnp.where(mine, near[slot, rows, :], far[slot, rows, :]).astype(F32),
            )

    over(heads // chunks, body)


def call(kernel, ins, outs, args, flops, scratch=()):
    place = {
        "s": pl.BlockSpec(memory_space=pltpu.SMEM),
        "v": pl.BlockSpec(memory_space=pltpu.VMEM),
    }
    total = sum(a.size * a.dtype.itemsize for a in args) + sum(
        o.size * o.dtype.itemsize for o in outs
    )
    return pl.pallas_call(
        kernel,
        in_specs=[place[kind] for kind in ins],
        out_specs=[place["v"] for _ in outs],
        out_shape=list(outs),
        scratch_shapes=list(scratch),
        cost_estimate=pl.CostEstimate(flops=flops, bytes_accessed=total, transcendentals=0),
    )(*args)


def grid_call(kernel, scal, first, steps, ins, outs, args, flops, scratch=(), alias=None):
    def spec(kind, array):
        shape = array.shape
        base = first if kind.islower() else 0
        zeros = (0,) * (len(shape) - 1)
        if kind in "cC":
            return pl.BlockSpec((shape[0], HB * 128), lambda h, sc: (0, h + base))
        if kind in "hH":
            return pl.BlockSpec((HB,) + shape[1:], lambda h, sc: (h + base,) + zeros)
        if kind == "p":
            return pl.BlockSpec((1,) + shape[1:], lambda h, sc: (h + base,) + zeros)
        if kind == "x":
            return pl.BlockSpec(
                (HB,) + shape[1:],
                lambda h, sc: (((h // (steps // 2)) ^ sc[4]) * (steps // 2) + h % (steps // 2),) + zeros,
            )
        if kind == "n":
            return pl.BlockSpec(memory_space=pl.ANY)
        return pl.BlockSpec(shape, lambda h, sc: (0,) + zeros)

    total = sum(a.size * a.dtype.itemsize for a in args) + sum(
        o.size * o.dtype.itemsize for _, o in outs
    )
    return pl.pallas_call(
        kernel,
        grid_spec=pltpu.PrefetchScalarGridSpec(
            num_scalar_prefetch=1,
            grid=(steps,),
            in_specs=[spec(kind, a) for kind, a in zip(ins, args)],
            out_specs=[spec(kind, o) for kind, o in outs],
            scratch_shapes=list(scratch),
        ),
        out_shape=[o for _, o in outs],
        input_output_aliases=alias or {},
        cost_estimate=pl.CostEstimate(flops=flops, bytes_accessed=total, transcendentals=0),
    )(scal, *args)


def total_paired(array):
    pairs = [(i, i ^ 1) for i in range(8)]
    columns = [[x + 2 * z for z in range(4)] for x in range(2)]
    got = lax.ppermute(array[4:], "ctx", pairs)
    half = (array[:4].astype(F32) + got.astype(F32)).astype(BF)
    parts = lax.all_to_all(half, "ctx", 0, 0, tiled=True, axis_index_groups=columns)
    piece = jnp.sum(parts.astype(F32), axis=0).astype(BF)
    wide = jnp.broadcast_to(piece[None], half.shape)
    column = lax.all_to_all(wide, "ctx", 0, 0, tiled=True, axis_index_groups=columns)
    other = lax.ppermute(column, "ctx", pairs)
    return column, other


def total_exchanged(array, count):
    shape = array.shape
    flat = array.reshape(count, -1, shape[-1])
    parts = lax.all_to_all(flat, "ctx", 0, 0, tiled=True)
    piece = jnp.sum(parts.astype(F32), axis=0).astype(BF)
    wide = jnp.broadcast_to(piece[None], (count,) + piece.shape)
    parts = lax.all_to_all(wide, "ctx", 0, 0, tiled=True)
    return parts.reshape(shape)


def local(query_rows, key_rows, value_rows, frequencies, norm_gain, out_grad, global_ids):
    count = lax.axis_size("ctx")
    pos = lax.axis_index("ctx").astype(jnp.int32)
    n, width = query_rows.shape
    heads, m, dh = frequencies.shape
    blk = n // BPD
    reach = (WIN - 1) * blk
    paired = count == 8 and heads == 16
    x, z = pos % 2, pos // 2
    sds = jax.ShapeDtypeStruct
    unit = 2 * n * m * dh * heads
    ids = global_ids.astype(jnp.int32)
    scal = jnp.stack([pos, ids[0], ids[1], jnp.int32(count - 1), x, z])
    gain = norm_gain.reshape(1, width)
    forth = [(i, i + 1) for i in range(count - 1)]
    back = [(i + 1, i) for i in range(count - 1)]
    masks = [pltpu.VMEM((n, n), F32), pltpu.VMEM((reach + 2 * blk, n), F32)]

    (glob,) = call(
        gather_kernel, "svv", [sds((heads // 2, 4 * blk, 2 * dh), BF)],
        (scal, key_rows, value_rows), unit // 16,
    )
    glob = total_exchanged(glob, count)
    kp = lax.ppermute(key_rows[n - reach :], "ctx", forth)
    vp = lax.ppermute(value_rows[n - reach :], "ctx", forth)
    qn = lax.ppermute(query_rows[:reach], "ctx", back)

    qf, kf = call(
        feat_kernel, "vvv", [sds((heads, n, m), BF), sds((heads, n, m), BF)],
        (query_rows, key_rows, frequencies), 2 * unit,
    )
    steps = heads // HB
    att, kfe, rows, sums = grid_call(
        forward_kernel, scal, 0, steps, "hhccpchcc",
        [
            ("h", sds((heads, dh, n), F32)),
            ("h", sds((heads, reach + 2 * blk, m), BF)),
            ("h", sds((heads, 8, n), F32)),
            ("a", sds((2, n), F32)),
        ],
        (qf, kf, kp, vp, glob, value_rows, frequencies, out_grad, gain),
        6 * unit, masks,
    )
    sums = lax.psum(sums, "head")
    ng, ngs, dg, gp = call(
        norm_kernel, "vvvvv",
        [
            sds((n, width), BF),
            sds((reach + PAD, width), BF),
            sds((heads, 1, n), F32),
            sds((heads, 1, dh), F32),
        ],
        (sums, rows, att, out_grad, gain), unit // 16,
    )
    ngn = lax.ppermute(ngs, "ctx", back)
    zrows = m + 4 * blk + PAD
    chunks = 2 if paired else 1
    per = steps // chunks
    gathered = []
    outs = [
        ("c", sds((n, width), BF)),
        ("c", sds((n, width), F32)),
        ("c", sds((n, width), F32)),
        ("x" if paired else "H", sds((heads // chunks, zrows, dh), BF)),
    ]
    held = ()
    for c in range(chunks):
        args = (query_rows, key_rows, kp, vp, glob, value_rows, qf, kf, kfe, ng, dg, gp, frequencies)
        body = backward_kernel
        if held:
            body = lambda *refs: backward_kernel(*refs[:14], *refs[17:])
        *held, zc = grid_call(
            body, scal, c * per, per, "ccccpchhhchhh" + "n" * len(held), outs, args + tuple(held),
            16 * unit // chunks, masks,
            {14 + i: i for i in range(len(held))},
        )
        if paired:
            gathered += total_paired(zc)
        else:
            gathered.append(total_exchanged(zc, count)[None])
    qg, kpart, vpart = held
    kpart, vpart = grid_call(
        next_kernel, scal, 0, steps, "cccchhcc",
        [("c", sds((n, width), F32)), ("c", sds((n, width), F32))],
        (qn, ngn, key_rows, value_rows, kf, frequencies, kpart, vpart),
        5 * unit, [pltpu.VMEM((n, reach), F32)],
    )
    kgrad, vgrad, fgrad, gain_grad = call(
        add_kernel, "s" + "v" * (2 + len(gathered)),
        [
            sds((n, width), BF),
            sds((n, width), BF),
            sds((heads, m, dh), F32),
            sds((heads, 1, dh), F32),
        ],
        (scal, kpart, vpart, *gathered), unit // 64,
    )
    return (qg, kgrad, vgrad, fgrad, gain_grad.reshape(-1))


def solution(mesh):
    strips = P("ctx", "head")

    return jax.shard_map(
        local,
        mesh=mesh,
        in_specs=(strips, strips, strips, P("head", None, None), P("head"), strips, P()),
        out_specs=(strips, strips, strips, P("head", None, None), P("head")),
        check_vma=False,
    )
```

```python
import jax
import jax.numpy as jnp
from jax import lax
from jax.experimental import pallas as pl
from jax.experimental.pallas import tpu as pltpu
from jax.sharding import PartitionSpec as P


D = 8192
BPD = 4
WIN = 4
EPS = 1e-05
BF = jnp.bfloat16
F32 = jnp.float32
HB = 2
PAD = 16


def nt(a, b):
    return lax.dot_general(a, b, (((1,), (1,)), ((), ())), preferred_element_type=F32)


def nn(a, b):
    return lax.dot_general(a, b, (((1,), (0,)), ((), ())), preferred_element_type=F32)


def tn(a, b):
    return lax.dot_general(a, b, (((0,), (0,)), ((), ())), preferred_element_type=F32)


def feats(rows, freq):
    scale = rows.shape[-1] ** (-0.25)
    wide = rows.astype(F32)
    square = jnp.sum(wide * wide, axis=-1, keepdims=True)
    score = nt(rows, freq)
    return (
        jnp.exp(scale * score - (0.5 * scale * scale) * square) * freq.shape[0] ** (-0.5)
    ).astype(BF)


def block_of(shape, axis, length):
    return lax.broadcasted_iota(jnp.int32, shape, axis) // length


def keep(mask):
    return jnp.where(mask, 1.0, 0.0).astype(F32)


def fill_masks(sc_ref, own_ref, ext_ref):
    n = own_ref.shape[0]
    blk = n // BPD
    reach = (WIN - 1) * blk
    pos = sc_ref[0]
    own_ref[...] = keep(block_of((n, n), 0, blk) <= block_of((n, n), 1, blk))
    before = block_of((reach, n), 0, blk) >= block_of((reach, n), 1, blk)
    ext_ref[:reach, :] = keep(before & (pos > 0))
    shape = (2 * blk, n)
    target = jnp.where(block_of(shape, 0, blk) == 0, sc_ref[1], sc_ref[2])
    query = block_of(shape, 1, blk) + pos * BPD
    ext_ref[reach:, :] = keep((target > query) | (target <= query - WIN))


def masked(values, mask):
    return jnp.where(mask > 0.5, values, 0.0)


def over(count, body, unroll=1):
    def step(i, carry):
        for j in range(unroll):
            body(i * unroll + j)
        return carry

    lax.fori_loop(0, count // unroll, step, 0)


def lanes(h, dh):
    return pl.ds(pl.multiple_of(h * dh, dh), dh)


def gather_kernel(sc_ref, k_ref, v_ref, glob_ref):
    n = k_ref.shape[0]
    blk = n // BPD
    pieces, _, wide = glob_ref.shape
    pos = sc_ref[0]
    for g in range(2):
        at = sc_ref[1 + g] - pos * BPD
        here = (at >= 0) & (at < BPD)
        start = pl.multiple_of(jnp.clip(at, 0, BPD - 1) * blk, blk)
        for i, src in enumerate((k_ref, v_ref)):
            first = (2 * i + g) * blk
            for p in range(pieces):
                rows = src[pl.ds(start, blk), p * wide : (p + 1) * wide]
                glob_ref[p, first : first + blk, :] = jnp.where(here, rows, jnp.zeros_like(rows))


def feat_kernel(q_ref, k_ref, f_ref, qf_ref, kf_ref):
    heads, _, dh = f_ref.shape

    def body(h):
        freq = f_ref[h].astype(BF)
        qf_ref[h] = feats(q_ref[:, lanes(h, dh)], freq)
        kf_ref[h] = feats(k_ref[:, lanes(h, dh)], freq)

    over(heads, body, 2)


def forward_kernel(
    sc_ref, qf_ref, kf_ref, kp_ref, vp_ref, glob_ref, v_ref, f_ref, g_ref, gain_ref,
    att_ref, kfe_ref, rows_ref, sums_ref, own_ref, ext_ref,
):
    dh = f_ref.shape[2]
    reach = kp_ref.shape[0]
    half = glob_ref.shape[1] // 2

    @pl.when(pl.program_id(0) == 0)
    def _():
        fill_masks(sc_ref, own_ref, ext_ref)
        sums_ref[...] = jnp.zeros_like(sums_ref)

    for i in range(HB):
        freq = f_ref[i].astype(BF)
        cols = slice(i * dh, (i + 1) * dh)
        kfe_ref[i, :reach, :] = feats(kp_ref[:, cols], freq)
        kfe_ref[i, reach:, :] = feats(glob_ref[0, :half, cols], freq)
        qf = qf_ref[i]
        own = masked(nt(kf_ref[i], qf), own_ref[...])
        ext = masked(nt(kfe_ref[i], qf), ext_ref[...])
        den = jnp.sum(own, axis=0, keepdims=True) + jnp.sum(ext, axis=0, keepdims=True)
        ext = ext.astype(BF)
        num = (
            tn(v_ref[:, cols], own.astype(BF))
            + tn(vp_ref[:, cols], ext[:reach])
            + tn(glob_ref[0, half:, cols], ext[reach:])
        )
        att = num / den
        gg = (gain_ref[:, cols] * g_ref[:, cols].astype(F32)).T
        square = jnp.sum(att * att, axis=0, keepdims=True)
        product = jnp.sum(att * gg, axis=0, keepdims=True)
        att_ref[i] = att
        rows_ref[i, 0:1, :] = den
        rows_ref[i, 1:2, :] = square
        rows_ref[i, 2:3, :] = product
        rows_ref[i, 3:8, :] = jnp.zeros((5, den.shape[1]), F32)
        sums_ref[0:1, :] += square
        sums_ref[1:2, :] += product


def norm_kernel(
    sums_ref, rows_ref, att_ref, g_ref, gain_ref, ng_ref, ngs_ref, dg_ref, gp_ref
):
    heads, dh, _ = att_ref.shape
    alpha = lax.rsqrt(sums_ref[0:1, :] / D + EPS)
    beta = alpha * alpha * alpha * sums_ref[1:2, :] / D
    reach = ngs_ref.shape[0] - PAD

    def body(h):
        cols = lanes(h, dh)
        den = rows_ref[h, 0:1, :]
        att = att_ref[h]
        wide = g_ref[:, cols].astype(F32)
        gg = (gain_ref[:, cols] * wide).T
        ng = ((alpha * gg - att * beta) / den).T.astype(BF)
        dg = -(alpha * rows_ref[h, 2:3, :] - beta * rows_ref[h, 1:2, :]) / den
        ng_ref[:, cols] = ng
        dg_ref[h] = dg
        ngs_ref[:reach, cols] = ng[:reach]
        pieces = [jnp.broadcast_to(dg[:, j : j + dh], (PAD // 2, dh)) for j in (0, dh)]
        ngs_ref[reach:, cols] = jnp.concatenate(pieces, axis=0).astype(BF)
        gp_ref[h] = jnp.sum(wide * (att * alpha).T, axis=0, keepdims=True)

    over(heads, body, 2)


def row_grad(u, low, rows, freq, scale):
    return scale * nn(low, freq) - (scale * scale) * rows.astype(F32) * jnp.sum(
        u, axis=-1, keepdims=True
    )


def backward_kernel(
    sc_ref, q_ref, k_ref, kp_ref, vp_ref, glob_ref, v_ref, qf_ref, kf_ref, kfe_ref,
    ng_ref, dg_ref, gp_ref, f_ref,
    qg_ref, kpart_ref, vpart_ref, z_ref, own_ref, ext_ref,
):
    _, m, dh = f_ref.shape
    scale = dh ** (-0.25)
    reach = kp_ref.shape[0]
    ngl = glob_ref.shape[1] // 2

    @pl.when(pl.program_id(0) == 0)
    def _():
        fill_masks(sc_ref, own_ref, ext_ref)

    for i in range(HB):
        freq = f_ref[i].astype(BF)
        cols = slice(i * dh, (i + 1) * dh)
        qf, kf, kfe = qf_ref[i], kf_ref[i], kfe_ref[i]
        ng = ng_ref[:, cols]
        dg = dg_ref[i]
        own = masked(nt(kf, qf), own_ref[...]).astype(BF)
        vpart_ref[:, cols] = nn(own, ng)
        glob = masked(nt(kfe[reach:], qf), ext_ref[reach:, :]).astype(BF)
        z_ref[i, m + ngl : m + 2 * ngl, :] = nn(glob, ng).astype(BF)
        d_own = masked(nt(v_ref[:, cols], ng) + dg, own_ref[...]).astype(BF)
        d_prev = masked(nt(vp_ref[:, cols], ng) + dg, ext_ref[:reach, :]).astype(BF)
        d_glob = masked(nt(glob_ref[0, ngl:, cols], ng) + dg, ext_ref[reach:, :]).astype(BF)
        d_ext = jnp.concatenate([d_prev, d_glob], axis=0)
        qu = (tn(d_own, kf) + tn(d_ext, kfe)) * qf.astype(F32)
        ku = nn(d_own, qf) * kf.astype(F32)
        kue = nn(d_ext, qf) * kfe.astype(F32)
        qul, kul, kuel = qu.astype(BF), ku.astype(BF), kue.astype(BF)
        q, k, kp, kg = q_ref[:, cols], k_ref[:, cols], kp_ref[:, cols], glob_ref[0, :ngl, cols]
        qg_ref[:, cols] = row_grad(qu, qul, q, freq, scale).astype(BF)
        kpart_ref[:, cols] = row_grad(ku, kul, k, freq, scale)
        z_ref[i, 0:m, :] = (
            scale * (tn(qul, q) + tn(kul, k) + tn(kuel[:reach], kp) + tn(kuel[reach:], kg))
        ).astype(BF)
        z_ref[i, m : m + ngl, :] = row_grad(kue[reach:], kuel[reach:], kg, freq, scale).astype(BF)
        z_ref[i, m + 2 * ngl :, :] = jnp.broadcast_to(gp_ref[i], (PAD, dh)).astype(BF)


def next_kernel(
    sc_ref, qn_ref, ngn_ref, k_ref, v_ref, kf_ref, f_ref, kpart_ref, vpart_ref,
    kg_ref, vg_ref, mask_ref,
):
    dh = f_ref.shape[2]
    scale = dh ** (-0.25)
    reach = qn_ref.shape[0]
    n = k_ref.shape[0]
    blk = n // BPD

    @pl.when(pl.program_id(0) == 0)
    def _():
        after = block_of((n, reach), 0, blk) >= block_of((n, reach), 1, blk) + 1
        mask_ref[...] = keep(after & (sc_ref[0] < sc_ref[3]))

    for i in range(HB):
        freq = f_ref[i].astype(BF)
        cols = slice(i * dh, (i + 1) * dh)
        qf = feats(qn_ref[:, cols], freq)
        kf = kf_ref[i]
        ng = ngn_ref[:reach, cols]
        tail = ngn_ref[reach:, cols].astype(F32)
        dg = jnp.concatenate([tail[0:1], tail[PAD // 2 : PAD // 2 + 1]], axis=1)[:, :reach]
        pt = masked(nt(kf, qf), mask_ref[...]).astype(BF)
        dt = masked(nt(v_ref[:, cols], ng) + dg, mask_ref[...]).astype(BF)
        vg_ref[:, cols] = vpart_ref[:, cols] + nn(pt, ng)
        ku = nn(dt, qf) * kf.astype(F32)
        kg_ref[:, cols] = kpart_ref[:, cols] + row_grad(
            ku, ku.astype(BF), k_ref[:, cols], freq, scale
        )


def add_kernel(sc_ref, kpart_ref, vpart_ref, *refs):
    z_refs, (kg_ref, vg_ref, fq_ref, gp_ref) = refs[:-4], refs[-4:]
    heads, m, dh = fq_ref.shape
    n = kpart_ref.shape[0]
    blk = n // BPD
    pos = sc_ref[0]
    weights = [
        [jnp.where(sc_ref[1 + g] == pos * BPD + r, 1.0, 0.0).astype(F32) for g in range(2)]
        for r in range(BPD)
    ]

    def finish(h, tile):
        cols = lanes(h, dh)
        fq_ref[h] = tile(slice(0, m))
        part = [tile(slice(m + j * blk, m + (j + 1) * blk)) for j in range(4)]
        for r in range(BPD):
            w0, w1 = weights[r]
            rows = slice(r * blk, (r + 1) * blk)
            kg_ref[rows, cols] = (kpart_ref[rows, cols] + w0 * part[0] + w1 * part[1]).astype(BF)
            vg_ref[rows, cols] = (vpart_ref[rows, cols] + w0 * part[2] + w1 * part[3]).astype(BF)
        gp_ref[h] = tile(slice(m + 4 * blk, m + 4 * blk + 1))

    if len(z_refs) == 1:
        over(heads, lambda h: finish(h, lambda rows: z_refs[0][0, h, rows, :].astype(F32)))
        return
    chunks = len(z_refs) // 2

    def body(i):
        mine = (i // 4) == sc_ref[4]
        slot = lax.rem(sc_ref[5] - lax.rem(i, 4) + 4, 4)
        for c in range(chunks):
            near, far = z_refs[2 * c : 2 * c + 2]
            finish(
                i + c * (heads // chunks),
                lambda rows: jnp.where(mine, near[slot, rows, :], far[slot, rows, :]).astype(F32),
            )

    over(heads // chunks, body)


def call(kernel, ins, outs, args, flops, scratch=()):
    place = {
        "s": pl.BlockSpec(memory_space=pltpu.SMEM),
        "v": pl.BlockSpec(memory_space=pltpu.VMEM),
    }
    total = sum(a.size * a.dtype.itemsize for a in args) + sum(
        o.size * o.dtype.itemsize for o in outs
    )
    return pl.pallas_call(
        kernel,
        in_specs=[place[kind] for kind in ins],
        out_specs=[place["v"] for _ in outs],
        out_shape=list(outs),
        scratch_shapes=list(scratch),
        cost_estimate=pl.CostEstimate(flops=flops, bytes_accessed=total, transcendentals=0),
    )(*args)


def grid_call(kernel, scal, first, steps, ins, outs, args, flops, scratch=(), alias=None):
    def spec(kind, array):
        shape = array.shape
        base = first if kind.islower() else 0
        zeros = (0,) * (len(shape) - 1)
        if kind in "cC":
            return pl.BlockSpec((shape[0], HB * 128), lambda h, sc: (0, h + base))
        if kind in "hH":
            return pl.BlockSpec((HB,) + shape[1:], lambda h, sc: (h + base,) + zeros)
        if kind == "p":
            return pl.BlockSpec((1,) + shape[1:], lambda h, sc: (h + base,) + zeros)
        if kind == "x":
            return pl.BlockSpec(
                (HB,) + shape[1:],
                lambda h, sc: (((h // (steps // 2)) ^ sc[4]) * (steps // 2) + h % (steps // 2),) + zeros,
            )
        if kind == "n":
            return pl.BlockSpec(memory_space=pl.ANY)
        return pl.BlockSpec(shape, lambda h, sc: (0,) + zeros)

    total = sum(a.size * a.dtype.itemsize for a in args) + sum(
        o.size * o.dtype.itemsize for _, o in outs
    )
    return pl.pallas_call(
        kernel,
        grid_spec=pltpu.PrefetchScalarGridSpec(
            num_scalar_prefetch=1,
            grid=(steps,),
            in_specs=[spec(kind, a) for kind, a in zip(ins, args)],
            out_specs=[spec(kind, o) for kind, o in outs],
            scratch_shapes=list(scratch),
        ),
        out_shape=[o for _, o in outs],
        input_output_aliases=alias or {},
        cost_estimate=pl.CostEstimate(flops=flops, bytes_accessed=total, transcendentals=0),
    )(scal, *args)


def total_paired(array, z):
    pairs = [(i, i ^ 1) for i in range(8)]
    turn = {k: [(i, (i + 2 * k) % 8) for i in range(8)] for k in (1, 2, 3)}
    got = lax.ppermute(array[4:], "ctx", pairs)
    half = (array[:4].astype(F32) + got.astype(F32)).astype(BF)
    pick = lambda i: lax.dynamic_index_in_dim(half, i, 0, keepdims=False)
    sent = []
    for k in (2, 1, 3):
        sent.append(lax.ppermute(pick((z + k) % 4), "ctx", turn[k]))
    piece = (pick(z).astype(F32) + sum(s.astype(F32) for s in sent)).astype(BF)
    column = [piece]
    for k in (1, 2, 3):
        column.append(lax.ppermute(piece, "ctx", turn[k]))
    column = jnp.stack(column)
    other = lax.ppermute(column, "ctx", pairs)
    return column, other


def total_exchanged(array, count):
    shape = array.shape
    flat = array.reshape(count, -1, shape[-1])
    parts = lax.all_to_all(flat, "ctx", 0, 0, tiled=True)
    piece = jnp.sum(parts.astype(F32), axis=0).astype(BF)
    wide = jnp.broadcast_to(piece[None], (count,) + piece.shape)
    parts = lax.all_to_all(wide, "ctx", 0, 0, tiled=True)
    return parts.reshape(shape)


def local(query_rows, key_rows, value_rows, frequencies, norm_gain, out_grad, global_ids):
    count = lax.axis_size("ctx")
    pos = lax.axis_index("ctx").astype(jnp.int32)
    n, width = query_rows.shape
    heads, m, dh = frequencies.shape
    blk = n // BPD
    reach = (WIN - 1) * blk
    paired = count == 8 and heads == 16
    x, z = pos % 2, pos // 2
    sds = jax.ShapeDtypeStruct
    unit = 2 * n * m * dh * heads
    ids = global_ids.astype(jnp.int32)
    scal = jnp.stack([pos, ids[0], ids[1], jnp.int32(count - 1), x, z])
    gain = norm_gain.reshape(1, width)
    forth = [(i, i + 1) for i in range(count - 1)]
    back = [(i + 1, i) for i in range(count - 1)]
    masks = [pltpu.VMEM((n, n), F32), pltpu.VMEM((reach + 2 * blk, n), F32)]

    (glob,) = call(
        gather_kernel, "svv", [sds((heads // 2, 4 * blk, 2 * dh), BF)],
        (scal, key_rows, value_rows), unit // 16,
    )
    glob = total_exchanged(glob, count)
    kp = lax.ppermute(key_rows[n - reach :], "ctx", forth)
    vp = lax.ppermute(value_rows[n - reach :], "ctx", forth)
    qn = lax.ppermute(query_rows[:reach], "ctx", back)

    qf, kf = call(
        feat_kernel, "vvv", [sds((heads, n, m), BF), sds((heads, n, m), BF)],
        (query_rows, key_rows, frequencies), 2 * unit,
    )
    steps = heads // HB
    att, kfe, rows, sums = grid_call(
        forward_kernel, scal, 0, steps, "hhccpchcc",
        [
            ("h", sds((heads, dh, n), F32)),
            ("h", sds((heads, reach + 2 * blk, m), BF)),
            ("h", sds((heads, 8, n), F32)),
            ("a", sds((2, n), F32)),
        ],
        (qf, kf, kp, vp, glob, value_rows, frequencies, out_grad, gain),
        6 * unit, masks,
    )
    sums = lax.psum(sums, "head")
    ng, ngs, dg, gp = call(
        norm_kernel, "vvvvv",
        [
            sds((n, width), BF),
            sds((reach + PAD, width), BF),
            sds((heads, 1, n), F32),
            sds((heads, 1, dh), F32),
        ],
        (sums, rows, att, out_grad, gain), unit // 16,
    )
    ngn = lax.ppermute(ngs, "ctx", back)
    zrows = m + 4 * blk + PAD
    chunks = 2 if paired else 1
    per = steps // chunks
    gathered = []
    outs = [
        ("c", sds((n, width), BF)),
        ("c", sds((n, width), F32)),
        ("c", sds((n, width), F32)),
        ("x" if paired else "H", sds((heads // chunks, zrows, dh), BF)),
    ]
    held = ()
    for c in range(chunks):
        args = (query_rows, key_rows, kp, vp, glob, value_rows, qf, kf, kfe, ng, dg, gp, frequencies)
        body = backward_kernel
        if held:
            body = lambda *refs: backward_kernel(*refs[:14], *refs[17:])
        *held, zc = grid_call(
            body, scal, c * per, per, "ccccpchhhchhh" + "n" * len(held), outs, args + tuple(held),
            16 * unit // chunks, masks,
            {14 + i: i for i in range(len(held))},
        )
        if paired:
            gathered += total_paired(zc, z)
        else:
            gathered.append(total_exchanged(zc, count)[None])
    qg, kpart, vpart = held
    kpart, vpart = grid_call(
        next_kernel, scal, 0, steps, "cccchhcc",
        [("c", sds((n, width), F32)), ("c", sds((n, width), F32))],
        (qn, ngn, key_rows, value_rows, kf, frequencies, kpart, vpart),
        5 * unit, [pltpu.VMEM((n, reach), F32)],
    )
    kgrad, vgrad, fgrad, gain_grad = call(
        add_kernel, "s" + "v" * (2 + len(gathered)),
        [
            sds((n, width), BF),
            sds((n, width), BF),
            sds((heads, m, dh), F32),
            sds((heads, 1, dh), F32),
        ],
        (scal, kpart, vpart, *gathered), unit // 64,
    )
    return (qg, kgrad, vgrad, fgrad, gain_grad.reshape(-1))


def solution(mesh):
    strips = P("ctx", "head")

    return jax.shard_map(
        local,
        mesh=mesh,
        in_specs=(strips, strips, strips, P("head", None, None), P("head"), strips, P()),
        out_specs=(strips, strips, strips, P("head", None, None), P("head")),
        check_vma=False,
    )
```
